32 devices in a mesh: groups: 2 (over y), col: 4 (over z), row: 2 (over x), sub: 2 (over core).
Axes of the slice: x: 2, y: 2, z: 4, core: 2. Of those that a mesh axis runs over, the one named last changes fastest.
Arguments:
- pair: float32 [16, 256, 128], P(('groups', 'row', 'sub'), 'col'), parts along dimension 0, may hold values from -6 to 6
- w_query: float32 [128, 128], replicated, may hold values from -0.5 to 0.5
- w_key: float32 [128, 128], replicated, may hold values from -0.5 to 0.5
- w_value: float32 [128, 128], replicated, may hold values from -0.5 to 0.5
- bias: bfloat16 [8, 256, 256], P('groups', 'col', ('row', 'sub')), parts along dimension 0, may hold values from -6 to 6
- grad_out: float32 [16, 256, 128], P(('groups', 'row', 'sub'), 'col'), parts along dimension 0, may hold values from -6 to 6
- log_total: float32 [4, 16, 256], P(None, ('groups', 'row', 'sub'), 'col'), parts along dimension 1, may hold values from 7 to 9
- row_corr: float32 [4, 16, 256], P(None, ('groups', 'row', 'sub'), 'col'), parts along dimension 1, may hold values from -3 to 3
Outputs:
- query_grad: float32 [16, 256, 128], P(('groups', 'row', 'sub'), 'col'), parts along dimension 0
- key_pair_grad: float32 [16, 256, 128], P(('groups', 'row', 'sub'), 'col'), parts along dimension 0
- bias_grad: float32 [8, 256, 256], P('groups', 'col', ('row', 'sub')), parts along dimension 0
The draws below stay inside these ranges and needn't reach their ends.
There are 2 independent parts, one for each index of `groups`. The reference program is written for one: setup_inputs(seed, part) draws one part's arguments, and reference() takes and returns one part's arrays. A program takes and returns all parts, laid end to end along the dimension named above; an argument that names none is the same for every part. Nothing has to cross between parts.
All inputs are finite; a program needn't handle non-finite values.
Results may differ from the reference program's by a relative error of at most 0.0003.
Values may be sent and summed in bfloat16 or wider, within the bound.
No kernel may reach another device: no remote copies, remote signals or barrier semaphores. Data moves between devices by JAX's collectives and lax.ppermute only.
A program may use at most 64 MiB of HBM per device.

```python
import jax
import jax.numpy as jnp
from jax import lax

C = 128
H = 4
DH = 32
HD = 128
N = 256
NI = 8


def block_scale(key, shape, split, smallest, high):
    level = 1.0
    for position, blocks in split:
        heights = jax.random.uniform(jax.random.fold_in(jax.random.fold_in(key, 6), position), (blocks,), jnp.float32, smallest / len(split), high / len(split))
        level = level * jnp.repeat(jnp.exp(heights), shape[position] // blocks).reshape((-1,) + (1,) * (len(shape) - 1 - position))
    return level


def normal_values(stream_key, extent, spread, reach, split=(), kind=jnp.bfloat16):
    array = jax.random.normal(stream_key, extent, jnp.float32) * spread
    if len(split) > 0:
        array = block_scale(stream_key, extent, split, -0.22, 0.18) * array
    return jnp.clip(array, min=-reach, max=reach).astype(kind)


def setup_inputs(seed: int = 0, part: int = 0) -> dict:
    seeds = jax.random.split(jax.random.key(seed), 9)
    part_keys = jax.random.split(jax.random.fold_in(seeds[8], part), 9)
    pair = normal_values(part_keys[0], (NI, N, C), 1.0, 6.0, ((0, 4), (1, 4)), jnp.float32)
    w_query = normal_values(seeds[1], (C, HD), C ** -0.5, 0.5, (), jnp.float32)
    w_key = normal_values(seeds[2], (C, HD), C ** -0.5, 0.5, (), jnp.float32)
    w_value = normal_values(seeds[3], (C, HD), C ** -0.5, 0.5, (), jnp.float32)
    bias = normal_values(part_keys[4], (H, N, N), 1.0, 6.0, ((1, 4), (2, 4)))
    grad_out = normal_values(part_keys[5], (NI, N, HD), 1.0, 6.0, ((0, 4), (1, 4)), jnp.float32)
    log_total = jnp.clip(7.0 + 2.0 * jax.random.uniform(part_keys[6], (H, NI, N), jnp.float32) ** block_scale(part_keys[6], (H, NI, N), ((1, 4), (2, 4)), -0.2, 0.2), 7.0, 9.0)
    row_corr = normal_values(part_keys[7], (H, NI, N), 0.5, 3.0, ((1, 4), (2, 4)), jnp.float32)
    return {"pair": pair, "w_query": w_query, "w_key": w_key, "w_value": w_value, "bias": bias, "grad_out": grad_out, "log_total": log_total, "row_corr": row_corr}


HIGH = lax.Precision.HIGHEST


def one_row(pair_row, grad_row, lse_row, corr_row, bias_full, w_query, w_key, w_value):
    count = pair_row.shape[0]
    scale = DH ** -0.5
    query = jnp.dot(pair_row, w_query, precision=HIGH).reshape(count, H, DH)
    keys = jnp.dot(pair_row, w_key, precision=HIGH).reshape(count, H, DH)
    values = jnp.dot(pair_row, w_value, precision=HIGH).reshape(count, H, DH)
    grads = grad_row.reshape(count, H, DH)
    scores = jnp.einsum("jhd,khd->hjk", query, keys, precision=HIGH) * scale + bias_full
    probs = jnp.exp(scores - lse_row[:, :, None])
    dprobs = jnp.einsum("jhd,khd->hjk", grads, values, precision=HIGH)
    dscores = probs * (dprobs - corr_row[:, :, None])
    dquery = jnp.einsum("hjk,khd->jhd", dscores, keys, precision=HIGH) * scale
    dkeys = jnp.einsum("hjk,jhd->khd", dscores, query, precision=HIGH) * scale
    dvalues = jnp.einsum("hjk,jhd->khd", probs, grads, precision=HIGH)
    query_row = jnp.dot(dquery.reshape(count, HD), w_query.T, precision=HIGH)
    key_row = jnp.dot(dkeys.reshape(count, HD), w_key.T, precision=HIGH) + jnp.dot(dvalues.reshape(count, HD), w_value.T, precision=HIGH)
    return query_row, key_row, dscores


def reference(pair, w_query, w_key, w_value, bias, grad_out, log_total, row_corr):
    bias_full = bias.astype(jnp.float32)
    lse_rows = jnp.moveaxis(log_total, 1, 0)
    corr_rows = jnp.moveaxis(row_corr, 1, 0)

    def row_step(acc, row_items):
        query_row, key_row, dscores = one_row(row_items[0], row_items[1], row_items[2], row_items[3], bias_full, w_query, w_key, w_value)
        return acc + dscores, (query_row, key_row)

    total, (query_rows, key_rows) = lax.scan(row_step, jnp.zeros((H, N, N), jnp.float32), (pair, grad_out, lse_rows, corr_rows))
    return query_rows, key_rows, total
```

```python
import functools

import jax
import jax.numpy as jnp
from jax import lax
from jax.experimental import pallas as pl
from jax.experimental.pallas import tpu as pltpu
from jax.sharding import PartitionSpec as P

NN = (((1,), (0,)), ((), ()))
NT = (((1,), (1,)), ((), ()))
TN = (((0,), (0,)), ((), ()))


def split(x):
    high = x.astype(jnp.bfloat16)
    return high, (x - high.astype(jnp.float32)).astype(jnp.bfloat16)


def dot3(a, b, dims):
    def one(x, y):
        return lax.dot_general(x, y, dims, preferred_element_type=jnp.float32)

    return one(a[0], b[0]) + one(a[0], b[1]) + one(a[1], b[0])


def attend(where_ref, *refs, count, heads, head_dim):
    blocks = refs[:count]
    biases = refs[count : 2 * count]
    wq_ref, wk_ref, wv_ref, grad_ref, lse_ref, corr_ref = refs[2 * count : 2 * count + 6]
    query_ref, own_ref = refs[2 * count + 6 : 2 * count + 8]
    terms_refs = refs[2 * count + 8 : 3 * count + 7]
    dbias_ref = refs[3 * count + 7]
    bias_scr = refs[3 * count + 8]
    rows, cols, width = blocks[0].shape
    proj = heads * head_dim
    wide = heads * cols
    scale = head_dim ** (-0.5)
    shift = where_ref[0]

    wq = split(wq_ref[...])
    wk = split(wk_ref[...])
    wv = split(wv_ref[...])
    for slot in range(count):
        for head in range(heads):
            bias_scr[slot, :, head * cols : (head + 1) * cols] = biases[slot][head].astype(jnp.float32)

    lane_head = lax.broadcasted_iota(jnp.int32, (cols, wide), 1) // cols

    def widen(ref, row):
        stack = jnp.concatenate([ref[head, row : row + 1, :] for head in range(heads)], axis=0)
        stack = jnp.concatenate([stack, jnp.zeros((8 - heads % 8, cols), jnp.float32)], axis=0)
        turned = stack.T
        out = jnp.broadcast_to(turned[:, 0:1], (cols, wide))
        for head in range(1, heads):
            out = jnp.where(lane_head == head, turned[:, head : head + 1], out)
        return out

    row_head = lax.broadcasted_iota(jnp.int32, (wide, proj), 0) // cols
    chan_head = lax.broadcasted_iota(jnp.int32, (wide, proj), 1) // head_dim
    diag = row_head == chan_head
    fold_mask = lax.broadcasted_iota(jnp.int32, (cols, proj), 1) // head_dim

    def spread(pieces):
        return tuple(
            jnp.where(diag, jnp.concatenate([p] * heads, axis=0), jnp.zeros((), p.dtype)) for p in pieces
        )

    def fold(x):
        out = x[:cols]
        for head in range(1, heads):
            out = jnp.where(fold_mask == head, x[head * cols : (head + 1) * cols], out)
        return out

    own = split(blocks[0][...].reshape(rows * cols, width))
    query = dot3(own, wq, NN) * scale
    qs = [split(query[r * cols : (r + 1) * cols]) for r in range(rows)]
    gs = [split(grad_ref[r]) for r in range(rows)]
    lse = [widen(lse_ref, r) for r in range(rows)]
    corr = [widen(corr_ref, r) for r in range(rows)]
    dquery = [None] * rows
    for slot in range(count):
        piece = own if slot == 0 else split(blocks[slot][...].reshape(rows * cols, width))
        key = dot3(piece, wk, NN)
        val = dot3(piece, wv, NN)
        index = shift ^ slot
        bias = bias_scr[index]
        total = None
        dks = []
        dvs = []
        for r in range(rows):
            kb = spread(split(key[r * cols : (r + 1) * cols]))
            vb = spread(split(val[r * cols : (r + 1) * cols]))
            probs = jnp.exp(dot3(qs[r], kb, NT) + bias - lse[r])
            ds = probs * (dot3(gs[r], vb, NT) - corr[r])
            total = ds if total is None else total + ds
            dsp = split(ds)
            part = dot3(dsp, kb, NN)
            dquery[r] = part if dquery[r] is None else dquery[r] + part
            dks.append(fold(dot3(dsp, qs[r], TN)))
            dvs.append(fold(dot3(split(probs), gs[r], TN)))
        term = dot3(split(jnp.concatenate(dks, axis=0)), wk, NT) + dot3(
            split(jnp.concatenate(dvs, axis=0)), wv, NT
        )
        dest = own_ref if slot == 0 else terms_refs[slot - 1]
        dest[...] = term.reshape(rows, cols, width)
        for head in range(heads):
            dbias_ref[index, head] = total[:, head * cols : (head + 1) * cols]
    dq = jnp.concatenate(dquery, axis=0) * scale
    query_ref[...] = dot3(split(dq), wq, NT).reshape(rows, cols, width)


def combine(*refs, count):
    own_ref, dbias_ref = refs[:2]
    terms = refs[2 : count + 1]
    dbs = refs[count + 1 : 2 * count]
    key_ref, bias_ref = refs[2 * count :]
    total = own_ref[...]
    for ref in terms:
        total = total + ref[...]
    key_ref[...] = total
    total = dbias_ref[0]
    for ref in dbs:
        total = total + ref[...]
    bias_ref[...] = total


def xor_pairs(size, mask):
    return [(i, i ^ mask) for i in range(size)]


def on_device(ncol, nrow, nsub, pair, w_query, w_key, w_value, bias, grad_out, log_total, row_corr):
    rows, cols, width = pair.shape
    heads = log_total.shape[0]
    head_dim = w_query.shape[1] // heads
    nrs = nrow * nsub
    count = ncol
    tile = ("row", "sub")
    blocks = [pair] + [lax.ppermute(pair, "col", xor_pairs(ncol, k)) for k in range(1, ncol)]
    biases = [bias] + [lax.ppermute(bias, tile, xor_pairs(nrs, k)) for k in range(1, nrs)]
    place = lax.axis_index("col") ^ (lax.axis_index("row") * nsub + lax.axis_index("sub"))
    f32 = jnp.float32
    part = jax.ShapeDtypeStruct((rows, cols, width), f32)
    vmem = pl.BlockSpec(memory_space=pltpu.VMEM)
    outs = pl.pallas_call(
        functools.partial(attend, count=count, heads=heads, head_dim=head_dim),
        out_shape=[part] * (count + 1) + [jax.ShapeDtypeStruct((nrs, heads, cols, cols), f32)],
        in_specs=[pl.BlockSpec(memory_space=pltpu.SMEM)] + [vmem] * (2 * count + 6),
        out_specs=[vmem] * (count + 2),
        scratch_shapes=[pltpu.VMEM((nrs, cols, heads * cols), f32)],
        name="attend",
    )(place.reshape(1), *blocks, *biases, w_query, w_key, w_value, grad_out, log_total, row_corr)
    query_grad, own = outs[:2]
    terms = outs[2 : count + 1]
    dbias = outs[count + 1]
    got = [lax.ppermute(terms[k - 1], "col", xor_pairs(ncol, k)) for k in range(1, ncol)]
    dgot = [lax.ppermute(dbias[k], tile, xor_pairs(nrs, k)) for k in range(1, nrs)]
    key_grad, bias_grad = pl.pallas_call(
        functools.partial(combine, count=count),
        out_shape=[part, jax.ShapeDtypeStruct((heads, cols, cols), f32)],
        in_specs=[vmem] * (2 * count),
        out_specs=[vmem] * 2,
        name="combine",
    )(own, dbias, *got, *dgot)
    return query_grad, key_grad, bias_grad


def solution(mesh):
    size = mesh.shape
    placed = (
        P(("groups", "row", "sub"), "col", None),
        P(),
        P(),
        P(),
        P("groups", "col", ("row", "sub")),
        P(("groups", "row", "sub"), "col", None),
        P(None, ("groups", "row", "sub"), "col"),
        P(None, ("groups", "row", "sub"), "col"),
    )
    return jax.shard_map(
        functools.partial(on_device, size["col"], size["row"], size["sub"]),
        mesh=mesh,
        in_specs=placed,
        out_specs=(
            P(("groups", "row", "sub"), "col", None),
            P(("groups", "row", "sub"), "col", None),
            P("groups", "col", ("row", "sub")),
        ),
        check_vma=False,
    )
```

```python
import functools

import jax
import jax.numpy as jnp
from jax import lax
from jax.experimental import pallas as pl
from jax.experimental.pallas import tpu as pltpu
from jax.sharding import PartitionSpec as P

NN = (((1,), (0,)), ((), ()))
NT = (((1,), (1,)), ((), ()))
TN = (((0,), (0,)), ((), ()))
F32 = jnp.float32
BF16 = jnp.bfloat16


def split(x):
    high = x.astype(BF16)
    return high, (x - high.astype(F32)).astype(BF16)


def dot3(a, b, dims):
    def one(x, y):
        return lax.dot_general(x, y, dims, preferred_element_type=F32)

    return one(a[0], b[0]) + one(a[0], b[1]) + one(a[1], b[0])


def pair_of(ref):
    return ref[0], ref[1]


def store(ref, pieces):
    ref[0] = pieces[0]
    ref[1] = pieces[1]


class Shape:
    def __init__(self, rows, cols, width, heads, head_dim):
        self.rows, self.cols, self.width = rows, cols, width
        self.heads, self.head_dim = heads, head_dim
        self.proj, self.wide, self.flat = heads * head_dim, heads * cols, rows * cols


def prep(pair_ref, wq_ref, wk_ref, wv_ref, grad_ref, lse_ref, corr_ref, *outs, s):
    q_out, g_out, wq_out, wk_out, wv_out, lse_out, corr_out, key_out, val_out = outs
    wq = split(wq_ref[...])
    wk = split(wk_ref[...])
    wv = split(wv_ref[...])
    store(wq_out, wq)
    store(wk_out, wk)
    store(wv_out, wv)
    own = split(pair_ref[...].reshape(s.flat, s.width))
    store(q_out, split(dot3(own, wq, NN) * (s.head_dim ** (-0.5))))
    store(key_out, split(dot3(own, wk, NN)))
    store(val_out, split(dot3(own, wv, NN)))
    store(g_out, split(grad_ref[...].reshape(s.flat, s.proj)))
    lane_head = lax.broadcasted_iota(jnp.int32, (s.cols, s.wide), 1) // s.cols

    def widen(ref, row):
        stack = jnp.concatenate([ref[head, row : row + 1, :] for head in range(s.heads)], axis=0)
        stack = jnp.concatenate([stack, jnp.zeros((8 - s.heads % 8, s.cols), F32)], axis=0)
        turned = stack.T
        out = jnp.broadcast_to(turned[:, 0:1], (s.cols, s.wide))
        for head in range(1, s.heads):
            out = jnp.where(lane_head == head, turned[:, head : head + 1], out)
        return out

    for r in range(s.rows):
        lse_out[r] = widen(lse_ref, r)
        corr_out[r] = widen(corr_ref, r)


def process(s, refs, slots, bias_of, dquery):
    q_ref, g_ref, wk_ref, wv_ref, lse_ref, corr_ref = refs
    row_head = lax.broadcasted_iota(jnp.int32, (s.wide, s.proj), 0) // s.cols
    chan_head = lax.broadcasted_iota(jnp.int32, (s.wide, s.proj), 1) // s.head_dim
    diag = row_head == chan_head
    fold_mask = lax.broadcasted_iota(jnp.int32, (s.cols, s.proj), 1) // s.head_dim

    def spread(pieces):
        return tuple(
            jnp.where(diag, jnp.concatenate([p] * s.heads, axis=0), jnp.zeros((), p.dtype)) for p in pieces
        )

    def fold(x):
        out = x[: s.cols]
        for head in range(1, s.heads):
            out = jnp.where(fold_mask == head, x[head * s.cols : (head + 1) * s.cols], out)
        return out

    def rows_of(pieces, r):
        return tuple(p[r * s.cols : (r + 1) * s.cols] for p in pieces)

    wk = pair_of(wk_ref)
    wv = pair_of(wv_ref)
    query = pair_of(q_ref)
    grads = pair_of(g_ref)
    for slot, keyval in slots:
        key, val = keyval(wk, wv)
        bias = bias_of(slot)
        total = None
        dks = []
        dvs = []
        for r in range(s.rows):
            qs = rows_of(query, r)
            gs = rows_of(grads, r)
            kb = spread(rows_of(key, r))
            vb = spread(rows_of(val, r))
            probs = jnp.exp(dot3(qs, kb, NT) + bias - lse_ref[r])
            ds = probs * (dot3(gs, vb, NT) - corr_ref[r])
            total = ds if total is None else total + ds
            dsp = split(ds)
            part = dot3(dsp, kb, NN)
            dquery[r] = part if dquery[r] is None else dquery[r] + part
            dks.append(fold(dot3(dsp, qs, TN)))
            dvs.append(fold(dot3(split(probs), gs, TN)))
        term = dot3(split(jnp.concatenate(dks, axis=0)), wk, NT) + dot3(
            split(jnp.concatenate(dvs, axis=0)), wv, NT
        )
        yield slot, term.reshape(s.rows, s.cols, s.width), total


def from_block(s, ref):
    def keyval(wk, wv):
        piece = split(ref[...].reshape(s.flat, s.width))
        return split(dot3(piece, wk, NN)), split(dot3(piece, wv, NN))

    return keyval


def near(where_ref, key_ref, val_ref, *refs, s, slots, nrs):
    common = refs[:6]
    blocks = refs[6 : 5 + slots]
    biases = refs[5 + slots : 5 + slots + nrs]
    bias_out, dq_out, *outs = refs[5 + slots + nrs :]
    terms, totals = outs[:slots], outs[slots:]
    for m in range(nrs):
        for head in range(s.heads):
            bias_out[m, :, head * s.cols : (head + 1) * s.cols] = biases[m][head].astype(F32)
    shift = where_ref[0]
    work = [(0, lambda wk, wv: (pair_of(key_ref), pair_of(val_ref)))]
    work += [(k, from_block(s, blocks[k - 1])) for k in range(1, slots)]
    dquery = [None] * s.rows
    for slot, term, total in process(s, common, work, lambda k: bias_out[shift ^ k], dquery):
        terms[slot][...] = term
        totals[slot][...] = total
    for r in range(s.rows):
        dq_out[r] = dquery[r]


def far(where_ref, bias_ref, dq_ref, *refs, s, done, count):
    common = refs[:6]
    totals = refs[6 : 6 + done]
    left = count - done
    blocks = refs[6 + done : 6 + done + left]
    dq_out, *outs = refs[6 + done + left : -1]
    spot = refs[-1]
    terms, dbs = outs[:left], outs[left:]
    shift = where_ref[0]
    for k in range(done):
        spot[shift ^ k] = totals[k][...]
    work = [(done + k, from_block(s, blocks[k])) for k in range(left)]
    dquery = [dq_ref[r] for r in range(s.rows)]
    for slot, term, total in process(s, common, work, lambda k: bias_ref[shift ^ k], dquery):
        terms[slot - done][...] = term
        spot[shift ^ slot] = total
    for r in range(s.rows):
        dq_out[r] = dquery[r]
    for m, ref in enumerate(dbs):
        for head in range(s.heads):
            ref[head] = spot[m, :, head * s.cols : (head + 1) * s.cols]


def tail(dq_ref, wq_ref, out_ref, *, s):
    dq = dq_ref[...].reshape(s.flat, s.proj) * (s.head_dim ** (-0.5))
    out_ref[...] = dot3(split(dq), pair_of(wq_ref), NT).reshape(s.rows, s.cols, s.width)


def add_up(*refs):
    total = refs[0][...]
    for ref in refs[1:-1]:
        total = total + ref[...]
    refs[-1][...] = total


def xor_pairs(size, mask):
    return [(i, i ^ mask) for i in range(size)]


def here(x):
    return pltpu.with_memory_space_constraint(x, pltpu.VMEM)


def call(body, outs, args, scratch=(), scalar=False):
    vmem = pl.BlockSpec(memory_space=pltpu.VMEM)
    specs = [vmem] * len(args)
    if scalar:
        specs[0] = pl.BlockSpec(memory_space=pltpu.SMEM)
    return pl.pallas_call(
        body,
        out_shape=outs,
        in_specs=specs,
        out_specs=[vmem] * len(outs),
        scratch_shapes=list(scratch),
        compiler_params=pltpu.CompilerParams(vmem_limit_bytes=16 << 20),
    )(*args)


NEAR = 2


def on_device(ncol, nrow, nsub, pair, w_query, w_key, w_value, bias, grad_out, log_total, row_corr):
    rows, cols, width = pair.shape
    heads = log_total.shape[0]
    s = Shape(rows, cols, width, heads, w_query.shape[1] // heads)
    nrs = nrow * nsub
    count = ncol
    tile = ("row", "sub")

    def move(x, axis, size, mask):
        return lax.ppermute(x, axis, xor_pairs(size, mask))

    part = jax.ShapeDtypeStruct((rows, cols, width), F32)
    vpart = pltpu.VMEM((rows, cols, width), F32)
    blocks = [here(move(pair, "col", ncol, k)) for k in range(1, ncol)]
    biases = [bias] + [here(move(bias, tile, nrs, k)) for k in range(1, nrs)]
    place = lax.axis_index("col") ^ (lax.axis_index("row") * nsub + lax.axis_index("sub"))
    place = place.reshape(1)
    two = pltpu.VMEM((2, s.flat, s.proj), BF16)
    wtwo = pltpu.VMEM((2, width, s.proj), BF16)
    wide = pltpu.VMEM((rows, cols, s.wide), F32)
    q, g, wq, wk, wv, lse, corr, key, val = map(
        here,
        call(
            functools.partial(prep, s=s),
            [two, two, wtwo, wtwo, wtwo, wide, wide, two, two],
            [pair, w_query, w_key, w_value, grad_out, log_total, row_corr],
        ),
    )
    common = [q, g, wk, wv, lse, corr]
    total = pltpu.VMEM((cols, s.wide), F32)
    dq_shape = pltpu.VMEM((rows, cols, s.proj), F32)
    bias_wide, dq, *rest = call(
        functools.partial(near, s=s, slots=NEAR, nrs=nrs),
        [pltpu.VMEM((nrs, cols, s.wide), F32), dq_shape] + [vpart] * NEAR + [total] * NEAR,
        [place, key, val, *common, *blocks[: NEAR - 1], *biases],
        scalar=True,
    )
    terms, totals = rest[:NEAR], rest[NEAR:]
    dbs = [pltpu.VMEM((heads, cols, cols), F32)] * nrs
    dq, *rest = call(
        functools.partial(far, s=s, done=NEAR, count=count),
        [dq_shape] + [vpart] * (count - NEAR) + dbs,
        [place, here(bias_wide), here(dq), *common, *map(here, totals), *blocks[NEAR - 1 :]],
        scratch=[pltpu.VMEM((nrs, cols, s.wide), F32)],
        scalar=True,
    )
    terms = terms + rest[: count - NEAR]
    dbias = rest[count - NEAR :]
    got = [here(move(terms[k], "col", ncol, k)) for k in range(1, ncol)]
    dgot = [here(move(dbias[k], tile, nrs, k)) for k in range(1, nrs)]
    (query_grad,) = call(functools.partial(tail, s=s), [part], [here(dq), wq])
    (key_grad,) = call(add_up, [part], [here(terms[0]), *got])
    (bias_grad,) = call(
        add_up, [jax.ShapeDtypeStruct((heads, cols, cols), F32)], [here(dbias[0]), *dgot]
    )
    return query_grad, key_grad, bias_grad


def solution(mesh):
    size = mesh.shape
    placed = (
        P(("groups", "row", "sub"), "col", None),
        P(),
        P(),
        P(),
        P("groups", "col", ("row", "sub")),
        P(("groups", "row", "sub"), "col", None),
        P(None, ("groups", "row", "sub"), "col"),
        P(None, ("groups", "row", "sub"), "col"),
    )
    return jax.shard_map(
        functools.partial(on_device, size["col"], size["row"], size["sub"]),
        mesh=mesh,
        in_specs=placed,
        out_specs=(
            P(("groups", "row", "sub"), "col", None),
            P(("groups", "row", "sub"), "col", None),
            P("groups", "col", ("row", "sub")),
        ),
        check_vma=False,
    )
```

```python
import functools

import jax
import jax.numpy as jnp
from jax import lax
from jax.experimental import pallas as pl
from jax.experimental.pallas import tpu as pltpu
from jax.sharding import PartitionSpec as P

NN = (((1,), (0,)), ((), ()))
NT = (((1,), (1,)), ((), ()))
TN = (((0,), (0,)), ((), ()))
F32 = jnp.float32
BF16 = jnp.bfloat16


def split(x):
    high = x.astype(BF16)
    return high, (x - high.astype(F32)).astype(BF16)


def dot3(a, b, dims):
    def one(x, y):
        return lax.dot_general(x, y, dims, preferred_element_type=F32)

    return one(a[0], b[0]) + one(a[0], b[1]) + one(a[1], b[0])


def pair_of(ref):
    return ref[0], ref[1]


def store(ref, pieces):
    ref[0] = pieces[0]
    ref[1] = pieces[1]


class Shape:
    def __init__(self, rows, cols, width, heads, head_dim):
        self.rows, self.cols, self.width = rows, cols, width
        self.heads, self.head_dim = heads, head_dim
        self.proj, self.wide, self.flat = heads * head_dim, heads * cols, rows * cols


def prep(*refs, s):
    sources, outs = refs[:7], refs[7:16]
    buffers, sem = refs[16:23], refs[23]
    copies = [pltpu.make_async_copy(src, dst, sem.at[i]) for i, (src, dst) in enumerate(zip(sources, buffers))]
    for copy in copies:
        copy.start()
    for copy in copies:
        copy.wait()
    pair_ref, wq_ref, wk_ref, wv_ref, grad_ref, lse_ref, corr_ref = buffers
    q_out, g_out, wq_out, wk_out, wv_out, lse_out, corr_out, key_out, val_out = outs
    wq = split(wq_ref[...])
    wk = split(wk_ref[...])
    wv = split(wv_ref[...])
    store(wq_out, wq)
    store(wk_out, wk)
    store(wv_out, wv)
    own = split(pair_ref[...].reshape(s.flat, s.width))
    store(q_out, split(dot3(own, wq, NN) * (s.head_dim ** (-0.5))))
    store(key_out, split(dot3(own, wk, NN)))
    store(val_out, split(dot3(own, wv, NN)))
    store(g_out, split(grad_ref[...].reshape(s.flat, s.proj)))
    lane_head = lax.broadcasted_iota(jnp.int32, (s.cols, s.wide), 1) // s.cols

    def widen(ref, row):
        stack = jnp.concatenate([ref[head, row : row + 1, :] for head in range(s.heads)], axis=0)
        stack = jnp.concatenate([stack, jnp.zeros((8 - s.heads % 8, s.cols), F32)], axis=0)
        turned = stack.T
        out = jnp.broadcast_to(turned[:, 0:1], (s.cols, s.wide))
        for head in range(1, s.heads):
            out = jnp.where(lane_head == head, turned[:, head : head + 1], out)
        return out

    for r in range(s.rows):
        lse_out[r] = widen(lse_ref, r)
        corr_out[r] = widen(corr_ref, r)


def process(s, refs, slots, bias_of, dquery):
    q_ref, g_ref, wk_ref, wv_ref, lse_ref, corr_ref = refs
    row_head = lax.broadcasted_iota(jnp.int32, (s.wide, s.proj), 0) // s.cols
    chan_head = lax.broadcasted_iota(jnp.int32, (s.wide, s.proj), 1) // s.head_dim
    diag = row_head == chan_head
    fold_mask = lax.broadcasted_iota(jnp.int32, (s.cols, s.proj), 1) // s.head_dim

    def spread(pieces):
        return tuple(
            jnp.where(diag, jnp.concatenate([p] * s.heads, axis=0), jnp.zeros((), p.dtype)) for p in pieces
        )

    def fold(x):
        out = x[: s.cols]
        for head in range(1, s.heads):
            out = jnp.where(fold_mask == head, x[head * s.cols : (head + 1) * s.cols], out)
        return out

    def rows_of(pieces, r):
        return tuple(p[r * s.cols : (r + 1) * s.cols] for p in pieces)

    wk = pair_of(wk_ref)
    wv = pair_of(wv_ref)
    query = pair_of(q_ref)
    grads = pair_of(g_ref)
    for slot, keyval in slots:
        key, val = keyval(wk, wv)
        bias = bias_of(slot)
        total = None
        dks = []
        dvs = []
        for r in range(s.rows):
            qs = rows_of(query, r)
            gs = rows_of(grads, r)
            kb = spread(rows_of(key, r))
            vb = spread(rows_of(val, r))
            probs = jnp.exp(dot3(qs, kb, NT) + bias - lse_ref[r])
            ds = probs * (dot3(gs, vb, NT) - corr_ref[r])
            total = ds if total is None else total + ds
            dsp = split(ds)
            part = dot3(dsp, kb, NN)
            dquery[r] = part if dquery[r] is None else dquery[r] + part
            dks.append(fold(dot3(dsp, qs, TN)))
            dvs.append(fold(dot3(split(probs), gs, TN)))
        term = dot3(split(jnp.concatenate(dks, axis=0)), wk, NT) + dot3(
            split(jnp.concatenate(dvs, axis=0)), wv, NT
        )
        yield slot, term, total


def from_block(s, ref):
    def keyval(wk, wv):
        piece = split(ref[...].reshape(s.flat, s.width))
        return split(dot3(piece, wk, NN)), split(dot3(piece, wv, NN))

    return keyval


LEVEL = 235.0


def encode(ref, x):
    rows, lanes = x.shape
    peak = jnp.max(jnp.max(jnp.abs(x), axis=1, keepdims=True), axis=0, keepdims=True)
    top = jnp.maximum(peak, 1e-30).astype(BF16)
    z = x * (LEVEL / top.astype(F32))
    z2 = z * z
    z4 = z2 * z2
    z8 = z4 * z4
    z16 = z8 * z8
    ref[0:rows] = jnp.where(x < 0, -z16, z16).astype(BF16)
    ref[rows : rows + 16] = jnp.broadcast_to(top, (16, lanes))


def decode(ref):
    rows = ref.shape[0] - 16
    code = ref[0:rows].astype(F32)
    top = ref[rows : rows + 16].astype(F32)[0:1]
    size = jnp.abs(code)
    for _ in range(4):
        size = jnp.sqrt(size)
    return jnp.where(code < 0, -size, size) * (top * (1.0 / LEVEL))


def pack(*refs, s, nsub):
    out = refs[-1]
    for m in range(nsub):
        for head in range(s.heads):
            out[m, :, head * s.cols : (head + 1) * s.cols] = refs[m][head]


def near(where_ref, key_ref, val_ref, *refs, s, slots, nrow, nsub):
    common = refs[:6]
    blocks = refs[6 : 5 + slots]
    packed = refs[5 + slots : 5 + slots + nrow]
    bias_out, dq_out, *outs = refs[5 + slots + nrow :]
    terms, totals = outs[:slots], outs[slots:]
    for m in range(nrow):
        bias_out[m * nsub : (m + 1) * nsub] = packed[m][...]
    shift = where_ref[0]
    work = [(0, lambda wk, wv: (pair_of(key_ref), pair_of(val_ref)))]
    work += [(k, from_block(s, blocks[k - 1])) for k in range(1, slots)]
    dquery = [None] * s.rows
    for slot, term, total in process(s, common, work, lambda k: bias_out[shift ^ k].astype(F32), dquery):
        if slot == 0:
            terms[0][...] = term
        else:
            encode(terms[slot], term)
        totals[slot][...] = total
    for r in range(s.rows):
        dq_out[r] = dquery[r]


def far(where_ref, bias_ref, dq_ref, *refs, s, done, count, nrow, nsub):
    common = refs[:6]
    totals = refs[6 : 6 + done]
    left = count - done
    blocks = refs[6 + done : 6 + done + left]
    dq_out, *outs = refs[6 + done + left : -1]
    spot = refs[-1]
    terms, dbs = outs[:left], outs[left:]
    shift = where_ref[0]
    for k in range(done):
        spot[shift ^ k] = totals[k][...]
    work = [(done + k, from_block(s, blocks[k])) for k in range(left)]
    dquery = [dq_ref[r] for r in range(s.rows)]
    for slot, term, total in process(s, common, work, lambda k: bias_ref[shift ^ k].astype(F32), dquery):
        encode(terms[slot - done], term)
        spot[shift ^ slot] = total
    for r in range(s.rows):
        dq_out[r] = dquery[r]
    for m in range(nrow * nsub):
        dbs[m % nsub][m // nsub] = spot[m]


def middle(*refs, nrow, nsub):
    parts, outs = refs[:nsub], refs[nsub:]
    for m in range(nrow):
        total = parts[0][m]
        for ref in parts[1:]:
            total = total + ref[m]
        if m == 0:
            outs[0][...] = total
        else:
            encode(outs[m], total)


def tail(dq_ref, wq_ref, out_ref, *, s):
    dq = dq_ref[...].reshape(s.flat, s.proj) * (s.head_dim ** (-0.5))
    out_ref[...] = dot3(split(dq), pair_of(wq_ref), NT).reshape(s.rows, s.cols, s.width)


def add_keys(own_ref, *refs, s):
    total = own_ref[...]
    for ref in refs[:-1]:
        total = total + decode(ref)
    refs[-1][...] = total.reshape(s.rows, s.cols, s.width)


def add_bias(own_ref, *refs, s):
    total = own_ref[...]
    for ref in refs[:-1]:
        total = total + decode(ref)
    for head in range(s.heads):
        refs[-1][head] = total[:, head * s.cols : (head + 1) * s.cols]


def xor_pairs(size, mask):
    return [(i, i ^ mask) for i in range(size)]


def here(x):
    return pltpu.with_memory_space_constraint(x, pltpu.VMEM)


def call(body, outs, args, scratch=(), scalar=False, kept=pltpu.VMEM):
    specs = [pl.BlockSpec(memory_space=pltpu.VMEM if kept is pltpu.VMEM else pl.ANY)] * len(args)
    vmem = pl.BlockSpec(memory_space=pltpu.VMEM)
    if scalar:
        specs[0] = pl.BlockSpec(memory_space=pltpu.SMEM)
    return pl.pallas_call(
        body,
        out_shape=outs,
        in_specs=specs,
        out_specs=[vmem] * len(outs),
        scratch_shapes=list(scratch),
        compiler_params=pltpu.CompilerParams(vmem_limit_bytes=16 << 20),
    )(*args)


NEAR = 2


def on_device(ncol, nrow, nsub, pair, w_query, w_key, w_value, bias, grad_out, log_total, row_corr):
    rows, cols, width = pair.shape
    heads = log_total.shape[0]
    s = Shape(rows, cols, width, heads, w_query.shape[1] // heads)
    nrs = nrow * nsub
    count = ncol

    def move(x, axis, size, mask):
        return lax.ppermute(x, axis, xor_pairs(size, mask))

    blocks = [here(move(pair, "col", ncol, k)) for k in range(1, ncol)]
    biases = [bias] + [here(move(bias, "sub", nsub, k)) for k in range(1, nsub)]
    packed_shape = pltpu.VMEM((nsub, cols, s.wide), BF16)
    (packed,) = call(functools.partial(pack, s=s, nsub=nsub), [packed_shape], biases)
    groups = [here(packed)] + [here(move(packed, "row", nrow, k)) for k in range(1, nrow)]
    place = lax.axis_index("col") ^ (lax.axis_index("row") * nsub + lax.axis_index("sub"))
    place = place.reshape(1)
    two = pltpu.VMEM((2, s.flat, s.proj), BF16)
    wtwo = pltpu.VMEM((2, width, s.proj), BF16)
    wide = pltpu.VMEM((rows, cols, s.wide), F32)
    params = [pair, w_query, w_key, w_value, grad_out, log_total, row_corr]
    q, g, wq, wk, wv, lse, corr, key, val = map(
        here,
        call(
            functools.partial(prep, s=s),
            [two, two, wtwo, wtwo, wtwo, wide, wide, two, two],
            [pltpu.with_memory_space_constraint(x, pltpu.HBM) for x in params],
            scratch=[pltpu.VMEM(x.shape, F32) for x in params]
            + [pltpu.SemaphoreType.DMA((len(params),))],
            kept=pltpu.HBM,
        ),
    )
    common = [q, g, wk, wv, lse, corr]
    total = pltpu.VMEM((cols, s.wide), F32)
    dq_shape = pltpu.VMEM((rows, cols, s.proj), F32)
    own_term = pltpu.VMEM((s.flat, width), F32)
    term = pltpu.VMEM((s.flat + 16, width), BF16)
    bias_wide, dq, *rest = call(
        functools.partial(near, s=s, slots=NEAR, nrow=nrow, nsub=nsub),
        [pltpu.VMEM((nrs, cols, s.wide), BF16), dq_shape, own_term]
        + [term] * (NEAR - 1)
        + [total] * NEAR,
        [place, key, val, *common, *blocks[: NEAR - 1], *groups],
        scalar=True,
    )
    terms, totals = rest[:NEAR], rest[NEAR:]
    dq, *rest = call(
        functools.partial(far, s=s, done=NEAR, count=count, nrow=nrow, nsub=nsub),
        [dq_shape] + [term] * (count - NEAR) + [pltpu.VMEM((nrow, cols, s.wide), F32)] * nsub,
        [place, here(bias_wide), here(dq), *common, *map(here, totals), *blocks[NEAR - 1 :]],
        scratch=[pltpu.VMEM((nrs, cols, s.wide), F32)],
        scalar=True,
    )
    terms = terms + rest[: count - NEAR]
    halves = rest[count - NEAR :]
    got = [here(move(terms[k], "col", ncol, k)) for k in range(1, ncol)]
    halves = [here(halves[0])] + [here(move(halves[k], "sub", nsub, k)) for k in range(1, nsub)]
    sums = call(
        functools.partial(middle, nrow=nrow, nsub=nsub),
        [total] + [pltpu.VMEM((cols + 16, s.wide), BF16)] * (nrow - 1),
        halves,
    )
    dgot = [here(move(sums[k], "row", nrow, k)) for k in range(1, nrow)]
    part = jax.ShapeDtypeStruct((rows, cols, width), F32)
    (query_grad,) = call(functools.partial(tail, s=s), [part], [here(dq), wq])
    (key_grad,) = call(functools.partial(add_keys, s=s), [part], [here(terms[0]), *got])
    dshape = jax.ShapeDtypeStruct((heads, cols, cols), F32)
    (bias_grad,) = call(functools.partial(add_bias, s=s), [dshape], [here(sums[0]), *dgot])
    return query_grad, key_grad, bias_grad


def solution(mesh):
    size = mesh.shape
    placed = (
        P(("groups", "row", "sub"), "col", None),
        P(),
        P(),
        P(),
        P("groups", "col", ("row", "sub")),
        P(("groups", "row", "sub"), "col", None),
        P(None, ("groups", "row", "sub"), "col"),
        P(None, ("groups", "row", "sub"), "col"),
    )
    return jax.shard_map(
        functools.partial(on_device, size["col"], size["row"], size["sub"]),
        mesh=mesh,
        in_specs=placed,
        out_specs=(
            P(("groups", "row", "sub"), "col", None),
            P(("groups", "row", "sub"), "col", None),
            P("groups", "col", ("row", "sub")),
        ),
        check_vma=False,
    )
```

```python
import functools

import jax
import jax.numpy as jnp
from jax import lax
from jax.experimental import pallas as pl
from jax.experimental.pallas import tpu as pltpu
from jax.sharding import PartitionSpec as P

NN = (((1,), (0,)), ((), ()))
NT = (((1,), (1,)), ((), ()))
TN = (((0,), (0,)), ((), ()))
F32 = jnp.float32
BF16 = jnp.bfloat16
LEVEL = 235.0


def split(x):
    high = x.astype(BF16)
    return high, (x - high.astype(F32)).astype(BF16)


def one(x, y, dims):
    return lax.dot_general(x, y, dims, preferred_element_type=F32)


def dot3(a, b, dims):
    axis = 0 if dims is NT else 1
    size = b[0].shape[axis]
    both = one(a[0], jnp.concatenate(b, axis=axis), dims)
    return both[:, :size] + both[:, size:] + one(a[1], b[0], dims)


def pair_of(ref, *index):
    return ref[(0, *index)], ref[(1, *index)]


def store(ref, pieces, *index):
    ref[(0, *index)] = pieces[0]
    ref[(1, *index)] = pieces[1]


class Shape:
    def __init__(self, rows, cols, width, heads, head_dim):
        self.rows, self.cols, self.width = rows, cols, width
        self.heads, self.head_dim = heads, head_dim
        self.proj, self.wide = heads * head_dim, heads * cols
        self.flat, self.two = rows * cols, 2 * cols


def encode(ref, x):
    rows, lanes = x.shape
    peak = jnp.max(jnp.max(jnp.abs(x), axis=1, keepdims=True), axis=0, keepdims=True)
    top = jnp.maximum(peak, 1e-30).astype(BF16)
    z = x * (LEVEL / top.astype(F32))
    z2 = z * z
    z4 = z2 * z2
    z8 = z4 * z4
    z16 = z8 * z8
    ref[0:rows] = jnp.where(x < 0, -z16, z16).astype(BF16)
    ref[rows : rows + 16] = jnp.broadcast_to(top, (16, lanes))


def decode(ref):
    rows = ref.shape[0] - 16
    code = ref[0:rows].astype(F32)
    top = ref[rows : rows + 16].astype(F32)[0:1]
    size = jnp.abs(code)
    for _ in range(4):
        size = jnp.sqrt(size)
    return jnp.where(code < 0, -size, size) * (top * (1.0 / LEVEL))


def half_join(low, high, width):
    lane = lax.broadcasted_iota(jnp.int32, low.shape, 1)
    return jnp.where(lane < width, low, high)


def pack(own_ref, other_ref, out_ref, *, s):
    out_ref[:, 0 : s.cols] = own_ref[...].reshape(s.wide, s.cols)
    out_ref[:, s.cols : s.two] = other_ref[...].reshape(s.wide, s.cols)


def prep(*refs, s):
    sources, outs = refs[:7], refs[7:14]
    buffers, sem = refs[14:21], refs[21]
    copies = [pltpu.make_async_copy(src, dst, sem.at[i]) for i, (src, dst) in enumerate(zip(sources, buffers))]
    for copy in copies:
        copy.start()
    for copy in copies:
        copy.wait()
    pair_ref, wq_ref, wk_ref, wv_ref, grad_ref, lse_ref, corr_ref = buffers
    q_out, g_out, wq_out, w_out, lse_out, corr_out, kv_out = outs
    wq = split(wq_ref[...])
    both = split(jnp.concatenate([wk_ref[...], wv_ref[...]], axis=1))
    store(wq_out, wq)
    store(w_out, both)
    own = split(pair_ref[...].reshape(s.flat, s.width))
    query = split(dot3(own, wq, NN) * (s.head_dim ** (-0.5)))
    kv_out[...] = dot3(own, both, NN)
    grads = split(grad_ref[...].reshape(s.flat, s.proj))
    row_head = lax.broadcasted_iota(jnp.int32, (s.wide, s.proj), 0) // s.cols
    chan_head = lax.broadcasted_iota(jnp.int32, (s.wide, s.proj), 1) // s.head_dim
    diag = row_head == chan_head

    def spread(piece):
        return jnp.where(diag, jnp.concatenate([piece] * s.heads, axis=0), jnp.zeros((), piece.dtype))

    def widen(ref, row):
        stack = jnp.concatenate([ref[head, row : row + 1, :] for head in range(s.heads)], axis=0)
        stack = jnp.concatenate([stack, jnp.zeros((8 - s.heads % 8, s.cols), F32)], axis=0)
        turned = stack.T
        return jnp.concatenate(
            [jnp.broadcast_to(turned[:, head : head + 1], (s.cols, s.two)) for head in range(s.heads)], axis=0
        )

    for r in range(s.rows):
        rows = slice(r * s.cols, (r + 1) * s.cols)
        store(q_out, [spread(x[rows]) for x in query], r)
        store(g_out, [spread(x[rows]) for x in grads], r)
        lse_out[r] = widen(lse_ref, r)
        corr_out[r] = widen(corr_ref, r)


def from_block(s, ref):
    return lambda both: dot3(split(ref[...].reshape(s.flat, s.width)), both, NN)


def scores(where_ref, *refs, s, pairs, own):
    q_ref, g_ref, w_ref, lse_ref, corr_ref = refs[:5]
    blocks = refs[5 : 5 + 2 * pairs]
    key_out, score_out, cot_out, kv_scr = refs[5 + 2 * pairs :]
    both = pair_of(w_ref)
    odd = where_ref[0] & 1
    for p in range(pairs):
        for slot in range(2):
            ref = blocks[2 * p + slot]
            value = ref[...] if own and p == 0 and slot == 0 else from_block(s, ref)(both)
            for r in range(s.rows):
                kv_scr[p, r, pl.ds((odd ^ slot) * s.cols, s.cols)] = value[r * s.cols : (r + 1) * s.cols]
        for r in range(s.rows):
            key = split(kv_scr[p, r, :, 0 : s.proj])
            val = split(kv_scr[p, r, :, s.proj : 2 * s.proj])
            store(key_out, key, p, r)
            score_out[p, r] = dot3(pair_of(q_ref, r), key, NT) - lse_ref[r]
            cot_out[p, r] = dot3(pair_of(g_ref, r), val, NT) - corr_ref[r]


def back(where_ref, *refs, s, nrow):
    q_ref, g_ref, w_ref = refs[:3]
    groups = refs[3 : 3 + nrow]
    sets = [refs[3 + nrow : 6 + nrow], refs[6 + nrow : 9 + nrow]]
    outs = refs[9 + nrow :]
    own_out, terms_out = outs[0], outs[1 : 2 * nrow]
    send_out, keep_out, dq_out, bias_scr, term_scr, spot = outs[2 * nrow :]
    shift = where_ref[0]
    odd = shift & 1
    both = pair_of(w_ref)
    for m, ref in enumerate(groups):
        bias_scr[m] = ref[...]
    dquery = [None] * s.rows
    for p in range(nrow):
        key_ref, score_ref, cot_ref = sets[min(p, 1)]
        at = max(p - 1, 0)
        group = (shift >> 1) ^ p
        bias = bias_scr[group].astype(F32)
        total = None
        grads = []
        for r in range(s.rows):
            query = pair_of(q_ref, r)
            cot = pair_of(g_ref, r)
            probs = jnp.exp(score_ref[at, r] + bias)
            ds = probs * cot_ref[at, r]
            total = ds if total is None else total + ds
            dsp = split(ds)
            part = dot3(dsp, pair_of(key_ref, at, r), NN)
            dquery[r] = part if dquery[r] is None else dquery[r] + part
            grads.append(jnp.concatenate([dot3(dsp, query, TN), dot3(split(probs), cot, TN)], axis=1))
        spot[group] = total
        term = dot3(split(jnp.concatenate(grads, axis=0)), both, NT)
        term_scr[p] = term.reshape(s.rows, s.two, s.width)
        for slot in range(2):
            value = jnp.concatenate(
                [term_scr[p, r, pl.ds((odd ^ slot) * s.cols, s.cols)] for r in range(s.rows)], axis=0
            )
            if p == 0 and slot == 0:
                own_out[...] = value
            else:
                encode(terms_out[2 * p + slot - 1], value)
    for r in range(s.rows):
        dq_out[r] = dquery[r]
    for p in range(nrow // 2):
        low, high = spot[2 * p], spot[2 * p + 1]
        keep_out[p] = half_join(low, pltpu.roll(high, s.cols, 1), s.cols)
        send_out[p] = half_join(pltpu.roll(low, s.cols, 1), high, s.cols)


def middle(keep_ref, got_ref, *outs, s, nrow):
    half = s.wide // 2
    for m in range(nrow):
        total = keep_ref[m // 2] + got_ref[m // 2]
        if m == 0:
            outs[0][...] = total
            continue
        top, bottom = total[:half], total[half:]
        if m % 2:
            top = pltpu.roll(top, s.cols, 1)
        else:
            bottom = pltpu.roll(bottom, s.cols, 1)
        encode(outs[m], half_join(top, bottom, s.cols))


def tail(dq_ref, wq_ref, out_ref, *, s):
    fold_mask = lax.broadcasted_iota(jnp.int32, (s.cols, s.proj), 1) // s.head_dim
    rows = []
    for r in range(s.rows):
        out = dq_ref[r, 0 : s.cols]
        for head in range(1, s.heads):
            out = jnp.where(fold_mask == head, dq_ref[r, head * s.cols : (head + 1) * s.cols], out)
        rows.append(out)
    dq = jnp.concatenate(rows, axis=0) * (s.head_dim ** (-0.5))
    out_ref[...] = dot3(split(dq), pair_of(wq_ref), NT).reshape(s.rows, s.cols, s.width)


def finish(own_ref, sum_ref, *refs, s, ncol, nrow):
    terms, parts = refs[: ncol - 1], refs[ncol - 1 : ncol + nrow - 2]
    key_out, bias_out = refs[ncol + nrow - 2 :]
    total = own_ref[...]
    for ref in terms:
        total = total + decode(ref)
    key_out[...] = total.reshape(s.rows, s.cols, s.width)
    total = None
    for ref in parts:
        value = decode(ref)
        total = value if total is None else total + value
    half = s.wide // 2
    whole = sum_ref[...]
    whole = jnp.concatenate([whole[:half] + total, whole[half:] + pltpu.roll(total, s.cols, 1)], axis=0)
    for head in range(s.heads):
        bias_out[head] = whole[head * s.cols : (head + 1) * s.cols, 0 : s.cols]


def xor_pairs(size, mask):
    return [(i, i ^ mask) for i in range(size)]


def here(x):
    return pltpu.with_memory_space_constraint(x, pltpu.VMEM)


def call(body, outs, args, scratch=(), scalar=False, inputs=pltpu.VMEM):
    specs = [pl.BlockSpec(memory_space=inputs)] * len(args)
    vmem = pl.BlockSpec(memory_space=pltpu.VMEM)
    if scalar:
        specs[0] = pl.BlockSpec(memory_space=pltpu.SMEM)
    return pl.pallas_call(
        body,
        out_shape=outs,
        in_specs=specs,
        out_specs=[vmem] * len(outs),
        scratch_shapes=list(scratch),
        compiler_params=pltpu.CompilerParams(vmem_limit_bytes=16 << 20),
    )(*args)


def on_device(ncol, nrow, nsub, pair, w_query, w_key, w_value, bias, grad_out, log_total, row_corr):
    if nsub != 2 or ncol != 2 * nrow:
        raise ValueError("mesh shape")
    rows, cols, width = pair.shape
    heads = log_total.shape[0]
    s = Shape(rows, cols, width, heads, w_query.shape[1] // heads)

    def move(x, axis, size, mask):
        return lax.ppermute(x, axis, xor_pairs(size, mask))

    blocks = [here(move(pair, "col", ncol, k)) for k in range(1, ncol)]
    other = here(move(bias, "sub", nsub, 1))
    (packed,) = call(functools.partial(pack, s=s), [pltpu.VMEM((s.wide, s.two), BF16)], [here(bias), other])
    groups = [here(packed)] + [here(move(packed, "row", nrow, k)) for k in range(1, nrow)]
    place = lax.axis_index("col") ^ (lax.axis_index("row") * nsub + lax.axis_index("sub"))
    place = place.reshape(1)
    spread = pltpu.VMEM((2, rows, s.wide, s.proj), BF16)
    wide = pltpu.VMEM((rows, s.wide, s.two), F32)
    params = [pair, w_query, w_key, w_value, grad_out, log_total, row_corr]
    q, g, wq, w_both, lse, corr, kv = map(
        here,
        call(
            functools.partial(prep, s=s),
            [
                spread,
                spread,
                pltpu.VMEM((2, width, s.proj), BF16),
                pltpu.VMEM((2, width, 2 * s.proj), BF16),
                wide,
                wide,
                pltpu.VMEM((s.flat, 2 * s.proj), F32),
            ],
            [pltpu.with_memory_space_constraint(x, pltpu.HBM) for x in params],
            scratch=[pltpu.VMEM(x.shape, F32) for x in params]
            + [pltpu.SemaphoreType.DMA((len(params),))],
            inputs=pl.ANY,
        ),
    )
    common = [q, g, w_both, lse, corr]
    total_shape = pltpu.VMEM((s.wide, s.two), F32)
    dq_shape = pltpu.VMEM((rows, s.wide, s.proj), F32)
    own_shape = pltpu.VMEM((s.flat, width), F32)
    term_shape = pltpu.VMEM((s.flat + 16, width), BF16)

    def score(members, pairs, own):
        grid = pltpu.VMEM((pairs, rows, s.wide, s.two), F32)
        outs = call(
            functools.partial(scores, s=s, pairs=pairs, own=own),
            [pltpu.VMEM((2, pairs, rows, s.two, s.proj), BF16), grid, grid],
            [place, *common, *members],
            scratch=[pltpu.VMEM((pairs, rows, s.two, 2 * s.proj), F32)],
            scalar=True,
        )
        return [here(x) for x in outs]

    sets = [*score([kv, blocks[0]], 1, True), *score(blocks[1:], nrow - 1, False)]
    ends = pltpu.VMEM((nrow // 2, s.wide, s.two), F32)
    own, *terms, send, keep, dq = call(
        functools.partial(back, s=s, nrow=nrow),
        [own_shape] + [term_shape] * (ncol - 1) + [ends, ends, dq_shape],
        [place, *common[:3], *groups, *sets],
        scratch=[
            pltpu.VMEM((nrow, s.wide, s.two), BF16),
            pltpu.VMEM((nrow, rows, s.two, width), F32),
            pltpu.VMEM((nrow, s.wide, s.two), F32),
        ],
        scalar=True,
    )
    got = [here(move(terms[k - 1], "col", ncol, k)) for k in range(1, ncol)]
    swapped = here(move(send, "sub", nsub, 1))
    summed, *sums = call(
        functools.partial(middle, s=s, nrow=nrow),
        [total_shape] + [pltpu.VMEM((s.wide // 2 + 16, s.two), BF16)] * (nrow - 1),
        [here(keep), swapped],
    )
    dgot = [here(move(sums[k - 1], "row", nrow, k)) for k in range(1, nrow)]
    part = jax.ShapeDtypeStruct((rows, cols, width), F32)
    (query_grad,) = call(functools.partial(tail, s=s), [part], [here(dq), wq])
    key_grad, bias_grad = call(
        functools.partial(finish, s=s, ncol=ncol, nrow=nrow),
        [part, jax.ShapeDtypeStruct((heads, cols, cols), F32)],
        [here(own), here(summed), *got, *dgot],
    )
    return query_grad, key_grad, bias_grad


def solution(mesh):
    size = mesh.shape
    placed = (
        P(("groups", "row", "sub"), "col", None),
        P(),
        P(),
        P(),
        P("groups", "col", ("row", "sub")),
        P(("groups", "row", "sub"), "col", None),
        P(None, ("groups", "row", "sub"), "col"),
        P(None, ("groups", "row", "sub"), "col"),
    )
    return jax.shard_map(
        functools.partial(on_device, size["col"], size["row"], size["sub"]),
        mesh=mesh,
        in_specs=placed,
        out_specs=(
            P(("groups", "row", "sub"), "col", None),
            P(("groups", "row", "sub"), "col", None),
            P("groups", "col", ("row", "sub")),
        ),
        check_vma=False,
    )
```

```python
import functools

import jax
import jax.numpy as jnp
from jax import lax
from jax.experimental import pallas as pl
from jax.experimental.pallas import tpu as pltpu
from jax.sharding import PartitionSpec as P

NN = (((1,), (0,)), ((), ()))
NT = (((1,), (1,)), ((), ()))
TN = (((0,), (0,)), ((), ()))
F32 = jnp.float32
BF16 = jnp.bfloat16
LEVEL = 235.0


def split(x):
    high = x.astype(BF16)
    return high, (x - high.astype(F32)).astype(BF16)


def one(x, y, dims):
    return lax.dot_general(x, y, dims, preferred_element_type=F32)


def dot3(a, b, dims):
    axis = 0 if dims is NT else 1
    size = b[0].shape[axis]
    both = one(a[0], jnp.concatenate(b, axis=axis), dims)
    return both[:, :size] + both[:, size:] + one(a[1], b[0], dims)


def pair_of(ref, *index):
    return ref[(0, *index)], ref[(1, *index)]


def store(ref, pieces, *index):
    ref[(0, *index)] = pieces[0]
    ref[(1, *index)] = pieces[1]


class Shape:
    def __init__(self, rows, cols, width, heads, head_dim):
        self.rows, self.cols, self.width = rows, cols, width
        self.heads, self.head_dim = heads, head_dim
        self.proj, self.wide = heads * head_dim, heads * cols
        self.flat, self.two = rows * cols, 2 * cols


def encode(ref, x):
    rows, lanes = x.shape
    peak = jnp.max(jnp.max(jnp.abs(x), axis=1, keepdims=True), axis=0, keepdims=True)
    top = jnp.maximum(peak, 1e-30).astype(BF16)
    z = x * (LEVEL / top.astype(F32))
    z2 = z * z
    z4 = z2 * z2
    z8 = z4 * z4
    z16 = z8 * z8
    ref[0:rows] = jnp.where(x < 0, -z16, z16).astype(BF16)
    ref[rows : rows + 16] = jnp.broadcast_to(top, (16, lanes))


def decode(ref):
    rows = ref.shape[0] - 16
    code = ref[0:rows].astype(F32)
    top = ref[rows : rows + 16].astype(F32)[0:1]
    size = jnp.exp2(jnp.log2(jnp.abs(code)) * 0.0625)
    return jnp.where(code < 0, -size, size) * (top * (1.0 / LEVEL))


def half_join(low, high, width):
    lane = lax.broadcasted_iota(jnp.int32, low.shape, 1)
    return jnp.where(lane < width, low, high)


def pack(own_ref, other_ref, out_ref, *, s):
    out_ref[:, 0 : s.cols] = own_ref[...].reshape(s.wide, s.cols)
    out_ref[:, s.cols : s.two] = other_ref[...].reshape(s.wide, s.cols)


def prep(*refs, s):
    sources, outs = refs[:7], refs[7:14]
    buffers, sem = refs[14:21], refs[21]
    copies = [pltpu.make_async_copy(src, dst, sem.at[i]) for i, (src, dst) in enumerate(zip(sources, buffers))]
    for copy in copies:
        copy.start()
    for copy in copies:
        copy.wait()
    pair_ref, wq_ref, wk_ref, wv_ref, grad_ref, lse_ref, corr_ref = buffers
    q_out, g_out, wq_out, w_out, lse_out, corr_out, kv_out = outs
    wq = split(wq_ref[...])
    both = split(jnp.concatenate([wk_ref[...], wv_ref[...]], axis=1))
    store(wq_out, wq)
    store(w_out, both)
    own = split(pair_ref[...].reshape(s.flat, s.width))
    query = split(dot3(own, wq, NN) * (s.head_dim ** (-0.5)))
    kv_out[...] = dot3(own, both, NN)
    grads = split(grad_ref[...].reshape(s.flat, s.proj))
    row_head = lax.broadcasted_iota(jnp.int32, (s.wide, s.proj), 0) // s.cols
    chan_head = lax.broadcasted_iota(jnp.int32, (s.wide, s.proj), 1) // s.head_dim
    diag = row_head == chan_head

    def spread(piece):
        return jnp.where(diag, jnp.concatenate([piece] * s.heads, axis=0), jnp.zeros((), piece.dtype))

    def widen(ref, row):
        stack = jnp.concatenate([ref[head, row : row + 1, :] for head in range(s.heads)], axis=0)
        stack = jnp.concatenate([stack, jnp.zeros((8 - s.heads % 8, s.cols), F32)], axis=0)
        turned = stack.T
        return jnp.concatenate(
            [jnp.broadcast_to(turned[:, head : head + 1], (s.cols, s.two)) for head in range(s.heads)], axis=0
        )

    for r in range(s.rows):
        rows = slice(r * s.cols, (r + 1) * s.cols)
        store(q_out, [spread(x[rows]) for x in query], r)
        store(g_out, [spread(x[rows]) for x in grads], r)
        lse_out[r] = widen(lse_ref, r)
        corr_out[r] = widen(corr_ref, r)


def from_block(s, ref):
    return lambda both: dot3(split(ref[...].reshape(s.flat, s.width)), both, NN)


def scores(where_ref, *refs, s, pairs, own):
    q_ref, g_ref, w_ref, lse_ref, corr_ref = refs[:5]
    blocks = refs[5 : 5 + 2 * pairs]
    key_out, score_out, cot_out, kv_scr = refs[5 + 2 * pairs :]
    both = pair_of(w_ref)
    odd = where_ref[0] & 1
    for p in range(pairs):
        for slot in range(2):
            ref = blocks[2 * p + slot]
            value = ref[...] if own and p == 0 and slot == 0 else from_block(s, ref)(both)
            for r in range(s.rows):
                kv_scr[p, r, pl.ds((odd ^ slot) * s.cols, s.cols)] = value[r * s.cols : (r + 1) * s.cols]
        for r in range(s.rows):
            key = split(kv_scr[p, r, :, 0 : s.proj])
            val = split(kv_scr[p, r, :, s.proj : 2 * s.proj])
            store(key_out, key, p, r)
            score_out[p, r] = dot3(pair_of(q_ref, r), key, NT) - lse_ref[r]
            cot_out[p, r] = dot3(pair_of(g_ref, r), val, NT) - corr_ref[r]


def back(where_ref, *refs, s, nrow):
    q_ref, g_ref, w_ref = refs[:3]
    groups = refs[3 : 3 + nrow]
    sets = [refs[3 + nrow : 6 + nrow], refs[6 + nrow : 9 + nrow]]
    outs = refs[9 + nrow :]
    own_out, terms_out = outs[0], outs[1 : 2 * nrow]
    send_out, keep_out, dq_out, bias_scr, term_scr, spot = outs[2 * nrow :]
    shift = where_ref[0]
    odd = shift & 1
    both = pair_of(w_ref)
    for m, ref in enumerate(groups):
        bias_scr[m] = ref[...]
    dquery = [None] * s.rows
    for p in range(nrow):
        key_ref, score_ref, cot_ref = sets[min(p, 1)]
        at = max(p - 1, 0)
        group = (shift >> 1) ^ p
        bias = bias_scr[group].astype(F32)
        total = None
        grads = []
        for r in range(s.rows):
            query = pair_of(q_ref, r)
            cot = pair_of(g_ref, r)
            probs = jnp.exp(score_ref[at, r] + bias)
            ds = probs * cot_ref[at, r]
            total = ds if total is None else total + ds
            dsp = split(ds)
            part = dot3(dsp, pair_of(key_ref, at, r), NN)
            dquery[r] = part if dquery[r] is None else dquery[r] + part
            grads.append(jnp.concatenate([dot3(dsp, query, TN), dot3(split(probs), cot, TN)], axis=1))
        spot[group] = total
        term = dot3(split(jnp.concatenate(grads, axis=0)), both, NT)
        term_scr[p] = term.reshape(s.rows, s.two, s.width)
        for slot in range(2):
            value = jnp.concatenate(
                [term_scr[p, r, pl.ds((odd ^ slot) * s.cols, s.cols)] for r in range(s.rows)], axis=0
            )
            if p == 0 and slot == 0:
                own_out[...] = value
            else:
                encode(terms_out[2 * p + slot - 1], value)
    for r in range(s.rows):
        dq_out[r] = dquery[r]
    for p in range(nrow // 2):
        low, high = spot[2 * p], spot[2 * p + 1]
        keep_out[p] = half_join(low, pltpu.roll(high, s.cols, 1), s.cols)
        send_out[p] = half_join(pltpu.roll(low, s.cols, 1), high, s.cols)


def middle(keep_ref, got_ref, *outs, s, nrow):
    half = s.wide // 2
    for m in range(nrow):
        total = keep_ref[m // 2] + got_ref[m // 2]
        if m == 0:
            outs[0][...] = total
            continue
        top, bottom = total[:half], total[half:]
        if m % 2:
            top = pltpu.roll(top, s.cols, 1)
        else:
            bottom = pltpu.roll(bottom, s.cols, 1)
        encode(outs[m], half_join(top, bottom, s.cols))


def tail(dq_ref, wq_ref, out_ref, *, s):
    fold_mask = lax.broadcasted_iota(jnp.int32, (s.cols, s.proj), 1) // s.head_dim
    rows = []
    for r in range(s.rows):
        out = dq_ref[r, 0 : s.cols]
        for head in range(1, s.heads):
            out = jnp.where(fold_mask == head, dq_ref[r, head * s.cols : (head + 1) * s.cols], out)
        rows.append(out)
    dq = jnp.concatenate(rows, axis=0) * (s.head_dim ** (-0.5))
    out_ref[...] = dot3(split(dq), pair_of(wq_ref), NT).reshape(s.rows, s.cols, s.width)


def finish(own_ref, sum_ref, *refs, s, ncol, nrow):
    terms, parts = refs[: ncol - 1], refs[ncol - 1 : ncol + nrow - 2]
    key_hbm, bias_hbm, key_out, bias_out, sem = refs[ncol + nrow - 2 :]
    total = own_ref[...]
    for ref in terms:
        total = total + decode(ref)
    key_out[...] = total.reshape(s.rows, s.cols, s.width)
    key_copy = pltpu.make_async_copy(key_out, key_hbm, sem.at[0])
    key_copy.start()
    total = None
    for ref in parts:
        value = decode(ref)
        total = value if total is None else total + value
    half = s.wide // 2
    whole = sum_ref[...]
    whole = jnp.concatenate([whole[:half] + total, whole[half:] + pltpu.roll(total, s.cols, 1)], axis=0)
    for head in range(s.heads):
        bias_out[head] = whole[head * s.cols : (head + 1) * s.cols, 0 : s.cols]
    bias_copy = pltpu.make_async_copy(bias_out, bias_hbm, sem.at[1])
    bias_copy.start()
    key_copy.wait()
    bias_copy.wait()


def xor_pairs(size, mask):
    return [(i, i ^ mask) for i in range(size)]


def here(x):
    return pltpu.with_memory_space_constraint(x, pltpu.VMEM)


def call(body, outs, args, scratch=(), scalar=False, inputs=pltpu.VMEM, outputs=pltpu.VMEM):
    specs = [pl.BlockSpec(memory_space=inputs)] * len(args)
    if scalar:
        specs[0] = pl.BlockSpec(memory_space=pltpu.SMEM)
    return pl.pallas_call(
        body,
        out_shape=outs,
        in_specs=specs,
        out_specs=[pl.BlockSpec(memory_space=outputs)] * len(outs),
        scratch_shapes=list(scratch),
        compiler_params=pltpu.CompilerParams(vmem_limit_bytes=16 << 20),
    )(*args)


def on_device(ncol, nrow, nsub, pair, w_query, w_key, w_value, bias, grad_out, log_total, row_corr):
    if nsub != 2 or ncol != 2 * nrow:
        raise ValueError("mesh shape")
    rows, cols, width = pair.shape
    heads = log_total.shape[0]
    s = Shape(rows, cols, width, heads, w_query.shape[1] // heads)

    def move(x, axis, size, mask):
        return lax.ppermute(x, axis, xor_pairs(size, mask))

    blocks = [here(move(pair, "col", ncol, k)) for k in range(1, ncol)]
    other = here(move(bias, "sub", nsub, 1))
    (packed,) = call(functools.partial(pack, s=s), [pltpu.VMEM((s.wide, s.two), BF16)], [here(bias), other])
    groups = [here(packed)] + [here(move(packed, "row", nrow, k)) for k in range(1, nrow)]
    place = lax.axis_index("col") ^ (lax.axis_index("row") * nsub + lax.axis_index("sub"))
    place = place.reshape(1)
    spread = pltpu.VMEM((2, rows, s.wide, s.proj), BF16)
    wide = pltpu.VMEM((rows, s.wide, s.two), F32)
    params = [pair, w_query, w_key, w_value, grad_out, log_total, row_corr]
    q, g, wq, w_both, lse, corr, kv = map(
        here,
        call(
            functools.partial(prep, s=s),
            [
                spread,
                spread,
                pltpu.VMEM((2, width, s.proj), BF16),
                pltpu.VMEM((2, width, 2 * s.proj), BF16),
                wide,
                wide,
                pltpu.VMEM((s.flat, 2 * s.proj), F32),
            ],
            [pltpu.with_memory_space_constraint(x, pltpu.HBM) for x in params],
            scratch=[pltpu.VMEM(x.shape, F32) for x in params]
            + [pltpu.SemaphoreType.DMA((len(params),))],
            inputs=pl.ANY,
        ),
    )
    common = [q, g, w_both, lse, corr]
    total_shape = pltpu.VMEM((s.wide, s.two), F32)
    dq_shape = pltpu.VMEM((rows, s.wide, s.proj), F32)
    own_shape = pltpu.VMEM((s.flat, width), F32)
    term_shape = pltpu.VMEM((s.flat + 16, width), BF16)

    def score(members, pairs, own):
        grid = pltpu.VMEM((pairs, rows, s.wide, s.two), F32)
        outs = call(
            functools.partial(scores, s=s, pairs=pairs, own=own),
            [pltpu.VMEM((2, pairs, rows, s.two, s.proj), BF16), grid, grid],
            [place, *common, *members],
            scratch=[pltpu.VMEM((pairs, rows, s.two, 2 * s.proj), F32)],
            scalar=True,
        )
        return [here(x) for x in outs]

    sets = [*score([kv, blocks[0]], 1, True), *score(blocks[1:], nrow - 1, False)]
    ends = pltpu.VMEM((nrow // 2, s.wide, s.two), F32)
    own, *terms, send, keep, dq = call(
        functools.partial(back, s=s, nrow=nrow),
        [own_shape] + [term_shape] * (ncol - 1) + [ends, ends, dq_shape],
        [place, *common[:3], *groups, *sets],
        scratch=[
            pltpu.VMEM((nrow, s.wide, s.two), BF16),
            pltpu.VMEM((nrow, rows, s.two, width), F32),
            pltpu.VMEM((nrow, s.wide, s.two), F32),
        ],
        scalar=True,
    )
    got = [here(move(terms[k - 1], "col", ncol, k)) for k in range(1, ncol)]
    swapped = here(move(send, "sub", nsub, 1))
    summed, *sums = call(
        functools.partial(middle, s=s, nrow=nrow),
        [total_shape] + [pltpu.VMEM((s.wide // 2 + 16, s.two), BF16)] * (nrow - 1),
        [here(keep), swapped],
    )
    dgot = [here(move(sums[k - 1], "row", nrow, k)) for k in range(1, nrow)]
    part = jax.ShapeDtypeStruct((rows, cols, width), F32)
    (query_grad,) = call(functools.partial(tail, s=s), [part], [here(dq), wq])
    key_grad, bias_grad = call(
        functools.partial(finish, s=s, ncol=ncol, nrow=nrow),
        [pltpu.HBM((rows, cols, width), F32), pltpu.HBM((heads, cols, cols), F32)],
        [here(own), here(summed), *got, *dgot],
        scratch=[
            pltpu.VMEM((rows, cols, width), F32),
            pltpu.VMEM((heads, cols, cols), F32),
            pltpu.SemaphoreType.DMA((2,)),
        ],
        outputs=pl.ANY,
    )
    return query_grad, key_grad, bias_grad


def solution(mesh):
    size = mesh.shape
    placed = (
        P(("groups", "row", "sub"), "col", None),
        P(),
        P(),
        P(),
        P("groups", "col", ("row", "sub")),
        P(("groups", "row", "sub"), "col", None),
        P(None, ("groups", "row", "sub"), "col"),
        P(None, ("groups", "row", "sub"), "col"),
    )
    return jax.shard_map(
        functools.partial(on_device, size["col"], size["row"], size["sub"]),
        mesh=mesh,
        in_specs=placed,
        out_specs=(
            P(("groups", "row", "sub"), "col", None),
            P(("groups", "row", "sub"), "col", None),
            P("groups", "col", ("row", "sub")),
        ),
        check_vma=False,
    )
```

```python
import functools

import jax
import jax.numpy as jnp
from jax import lax
from jax.experimental import pallas as pl
from jax.experimental.pallas import tpu as pltpu
from jax.sharding import PartitionSpec as P

NN = (((1,), (0,)), ((), ()))
NT = (((1,), (1,)), ((), ()))
TN = (((0,), (0,)), ((), ()))
F32 = jnp.float32
BF16 = jnp.bfloat16
LEVEL = 235.0


def split(x):
    high = x.astype(BF16)
    return high, (x - high.astype(F32)).astype(BF16)


def one(x, y, dims):
    return lax.dot_general(x, y, dims, preferred_element_type=F32)


def dot3(a, b, dims):
    axis = 0 if dims is NT else 1
    size = b[0].shape[axis]
    both = one(a[0], jnp.concatenate(b, axis=axis), dims)
    return both[:, :size] + both[:, size:] + one(a[1], b[0], dims)


def dot3_plain(a, b, dims):
    return one(a[0], b[0], dims) + one(a[0], b[1], dims) + one(a[1], b[0], dims)


def pair_of(ref, *index):
    return ref[(0, *index)], ref[(1, *index)]


def store(ref, pieces, *index):
    ref[(0, *index)] = pieces[0]
    ref[(1, *index)] = pieces[1]


class Shape:
    def __init__(self, rows, cols, width, heads, head_dim):
        self.rows, self.cols, self.width = rows, cols, width
        self.heads, self.head_dim = heads, head_dim
        self.proj, self.wide = heads * head_dim, heads * cols
        self.flat, self.two = rows * cols, 2 * cols


def encode(ref, x):
    rows, lanes = x.shape
    peak = jnp.max(jnp.max(jnp.abs(x), axis=1, keepdims=True), axis=0, keepdims=True)
    top = jnp.maximum(peak, 1e-30).astype(BF16)
    z = x * (LEVEL / top.astype(F32))
    z2 = z * z
    z4 = z2 * z2
    z8 = z4 * z4
    z16 = z8 * z8
    ref[0:rows] = jnp.where(x < 0, -z16, z16).astype(BF16)
    ref[rows : rows + 16] = jnp.broadcast_to(top, (16, lanes))


def decode(ref):
    rows = ref.shape[0] - 16
    code = ref[0:rows].astype(F32)
    top = ref[rows : rows + 16].astype(F32)[0:1]
    size = jnp.exp2(jnp.log2(jnp.abs(code)) * 0.0625)
    return jnp.where(code < 0, -size, size) * (top * (1.0 / LEVEL))


def half_join(low, high, width):
    lane = lax.broadcasted_iota(jnp.int32, low.shape, 1)
    return jnp.where(lane < width, low, high)


def pack(own_hbm, other_ref, out_ref, own_ref, sem, *, s):
    copy = pltpu.make_async_copy(own_hbm, own_ref, sem.at[0])
    copy.start()
    out_ref[:, s.cols : s.two] = other_ref[...].reshape(s.wide, s.cols)
    copy.wait()
    out_ref[:, 0 : s.cols] = own_ref[...].reshape(s.wide, s.cols)


def prep(*refs, s):
    sources, outs = refs[:7], refs[7:14]
    buffers, sem = refs[14:21], refs[21]
    copies = [pltpu.make_async_copy(src, dst, sem.at[i]) for i, (src, dst) in enumerate(zip(sources, buffers))]
    for copy in copies:
        copy.start()
    for copy in copies:
        copy.wait()
    pair_ref, wq_ref, wk_ref, wv_ref, grad_ref, lse_ref, corr_ref = buffers
    q_out, g_out, wq_out, w_out, lse_out, corr_out, kv_out = outs
    wq = split(wq_ref[...])
    both = split(jnp.concatenate([wk_ref[...], wv_ref[...]], axis=1))
    store(wq_out, wq)
    store(w_out, both)
    own = split(pair_ref[...].reshape(s.flat, s.width))
    query = split(dot3(own, wq, NN) * (s.head_dim ** (-0.5)))
    kv_out[...] = dot3(own, both, NN)
    grads = split(grad_ref[...].reshape(s.flat, s.proj))
    row_head = lax.broadcasted_iota(jnp.int32, (s.wide, s.proj), 0) // s.cols
    chan_head = lax.broadcasted_iota(jnp.int32, (s.wide, s.proj), 1) // s.head_dim
    diag = row_head == chan_head

    def spread(piece):
        return jnp.where(diag, jnp.concatenate([piece] * s.heads, axis=0), jnp.zeros((), piece.dtype))

    def widen(ref, row):
        stack = jnp.concatenate([ref[head, row : row + 1, :] for head in range(s.heads)], axis=0)
        stack = jnp.concatenate([stack, jnp.zeros((8 - s.heads % 8, s.cols), F32)], axis=0)
        turned = stack.T
        return jnp.concatenate(
            [jnp.broadcast_to(turned[:, head : head + 1], (s.cols, s.two)) for head in range(s.heads)], axis=0
        )

    for r in range(s.rows):
        rows = slice(r * s.cols, (r + 1) * s.cols)
        store(q_out, [spread(x[rows]) for x in query], r)
        store(g_out, [spread(x[rows]) for x in grads], r)
        lse_out[r] = widen(lse_ref, r)
        corr_out[r] = widen(corr_ref, r)


def from_block(s, ref):
    return lambda both: dot3_plain(split(ref[...].reshape(s.flat, s.width)), both, NN)


def scores(where_ref, *refs, s, pairs, own):
    q_ref, g_ref, w_ref, lse_ref, corr_ref = refs[:5]
    blocks = refs[5 : 5 + 2 * pairs]
    key_out, score_out, cot_out, kv_scr = refs[5 + 2 * pairs :]
    both = pair_of(w_ref)
    odd = where_ref[0] & 1
    for p in range(pairs):
        for slot in range(2):
            ref = blocks[2 * p + slot]
            value = ref[...] if own and p == 0 and slot == 0 else from_block(s, ref)(both)
            for r in range(s.rows):
                kv_scr[p, r, pl.ds((odd ^ slot) * s.cols, s.cols)] = value[r * s.cols : (r + 1) * s.cols]
        for r in range(s.rows):
            key = split(kv_scr[p, r, :, 0 : s.proj])
            val = split(kv_scr[p, r, :, s.proj : 2 * s.proj])
            store(key_out, key, p, r)
            score_out[p, r] = dot3_plain(pair_of(q_ref, r), key, NT) - lse_ref[r]
            cot_out[p, r] = dot3_plain(pair_of(g_ref, r), val, NT) - corr_ref[r]


def back(where_ref, *refs, s, nrow):
    q_ref, g_ref, w_ref = refs[:3]
    groups = refs[3 : 3 + nrow]
    sets = [refs[3 + nrow : 6 + nrow], refs[6 + nrow : 9 + nrow]]
    outs = refs[9 + nrow :]
    own_out, terms_out = outs[0], outs[1 : 2 * nrow]
    send_out, keep_out, dq_out, bias_scr, term_scr, spot = outs[2 * nrow :]
    shift = where_ref[0]
    odd = shift & 1
    both = pair_of(w_ref)
    for m, ref in enumerate(groups):
        bias_scr[m] = ref[...]
    dquery = [None] * s.rows
    for p in range(nrow):
        key_ref, score_ref, cot_ref = sets[min(p, 1)]
        at = max(p - 1, 0)
        group = (shift >> 1) ^ p
        bias = bias_scr[group].astype(F32)
        total = None
        grads = []
        for r in range(s.rows):
            query = pair_of(q_ref, r)
            cot = pair_of(g_ref, r)
            probs = jnp.exp(score_ref[at, r] + bias)
            ds = probs * cot_ref[at, r]
            total = ds if total is None else total + ds
            dsp = split(ds)
            part = dot3(dsp, pair_of(key_ref, at, r), NN)
            dquery[r] = part if dquery[r] is None else dquery[r] + part
            grads.append(jnp.concatenate([dot3(dsp, query, TN), dot3(split(probs), cot, TN)], axis=1))
        spot[group] = total
        term = dot3(split(jnp.concatenate(grads, axis=0)), both, NT)
        term_scr[p] = term.reshape(s.rows, s.two, s.width)
        for slot in range(2):
            value = jnp.concatenate(
                [term_scr[p, r, pl.ds((odd ^ slot) * s.cols, s.cols)] for r in range(s.rows)], axis=0
            )
            if p == 0 and slot == 0:
                own_out[...] = value
            else:
                encode(terms_out[2 * p + slot - 1], value)
    for r in range(s.rows):
        dq_out[r] = dquery[r]
    for p in range(nrow // 2):
        low, high = spot[2 * p], spot[2 * p + 1]
        keep_out[p] = half_join(low, pltpu.roll(high, s.cols, 1), s.cols)
        send_out[p] = half_join(pltpu.roll(low, s.cols, 1), high, s.cols)


def middle(keep_ref, got_ref, *outs, s, nrow):
    half = s.wide // 2
    for m in range(nrow):
        total = keep_ref[m // 2] + got_ref[m // 2]
        if m == 0:
            outs[0][...] = total
            continue
        top, bottom = total[:half], total[half:]
        if m % 2:
            top = pltpu.roll(top, s.cols, 1)
        else:
            bottom = pltpu.roll(bottom, s.cols, 1)
        encode(outs[m], half_join(top, bottom, s.cols))


def tail(dq_ref, wq_ref, out_ref, *, s):
    fold_mask = lax.broadcasted_iota(jnp.int32, (s.cols, s.proj), 1) // s.head_dim
    rows = []
    for r in range(s.rows):
        out = dq_ref[r, 0 : s.cols]
        for head in range(1, s.heads):
            out = jnp.where(fold_mask == head, dq_ref[r, head * s.cols : (head + 1) * s.cols], out)
        rows.append(out)
    dq = jnp.concatenate(rows, axis=0) * (s.head_dim ** (-0.5))
    out_ref[...] = dot3(split(dq), pair_of(wq_ref), NT).reshape(s.rows, s.cols, s.width)


def finish(own_ref, sum_ref, *refs, s, ncol, nrow):
    terms, parts = refs[: ncol - 1], refs[ncol - 1 : ncol + nrow - 2]
    key_hbm, bias_hbm, key_out, bias_out, sem = refs[ncol + nrow - 2 :]
    total = own_ref[...]
    for ref in terms:
        total = total + decode(ref)
    key_out[...] = total.reshape(s.rows, s.cols, s.width)
    key_copy = pltpu.make_async_copy(key_out, key_hbm, sem.at[0])
    key_copy.start()
    total = None
    for ref in parts:
        value = decode(ref)
        total = value if total is None else total + value
    half = s.wide // 2
    whole = sum_ref[...]
    whole = jnp.concatenate([whole[:half] + total, whole[half:] + pltpu.roll(total, s.cols, 1)], axis=0)
    for head in range(s.heads):
        bias_out[head] = whole[head * s.cols : (head + 1) * s.cols, 0 : s.cols]
    bias_copy = pltpu.make_async_copy(bias_out, bias_hbm, sem.at[1])
    bias_copy.start()
    key_copy.wait()
    bias_copy.wait()


def xor_pairs(size, mask):
    return [(i, i ^ mask) for i in range(size)]


def here(x):
    return pltpu.with_memory_space_constraint(x, pltpu.VMEM)


def call(body, outs, args, scratch=(), scalar=False, inputs=pltpu.VMEM, outputs=pltpu.VMEM, far_away=False):
    specs = [pl.BlockSpec(memory_space=inputs)] * len(args)
    if scalar:
        specs[0] = pl.BlockSpec(memory_space=pltpu.SMEM)
    if far_away:
        specs[0] = pl.BlockSpec(memory_space=pl.ANY)
    return pl.pallas_call(
        body,
        out_shape=outs,
        in_specs=specs,
        out_specs=[pl.BlockSpec(memory_space=outputs)] * len(outs),
        scratch_shapes=list(scratch),
        compiler_params=pltpu.CompilerParams(vmem_limit_bytes=16 << 20),
    )(*args)


def on_device(ncol, nrow, nsub, pair, w_query, w_key, w_value, bias, grad_out, log_total, row_corr):
    if nsub != 2 or ncol != 2 * nrow:
        raise ValueError("mesh shape")
    rows, cols, width = pair.shape
    heads = log_total.shape[0]
    s = Shape(rows, cols, width, heads, w_query.shape[1] // heads)

    def move(x, axis, size, mask):
        return lax.ppermute(x, axis, xor_pairs(size, mask))

    blocks = [here(move(pair, "col", ncol, k)) for k in range(1, ncol)]
    other = here(move(bias, "sub", nsub, 1))
    (packed,) = call(
        functools.partial(pack, s=s),
        [pltpu.VMEM((s.wide, s.two), BF16)],
        [pltpu.with_memory_space_constraint(bias, pltpu.HBM), other],
        scratch=[pltpu.VMEM(bias.shape, BF16), pltpu.SemaphoreType.DMA((1,))],
        far_away=True,
    )
    groups = [here(packed)] + [here(move(packed, "row", nrow, k)) for k in range(1, nrow)]
    place = lax.axis_index("col") ^ (lax.axis_index("row") * nsub + lax.axis_index("sub"))
    place = place.reshape(1)
    spread = pltpu.VMEM((2, rows, s.wide, s.proj), BF16)
    wide = pltpu.VMEM((rows, s.wide, s.two), F32)
    params = [pair, w_query, w_key, w_value, grad_out, log_total, row_corr]
    q, g, wq, w_both, lse, corr, kv = map(
        here,
        call(
            functools.partial(prep, s=s),
            [
                spread,
                spread,
                pltpu.VMEM((2, width, s.proj), BF16),
                pltpu.VMEM((2, width, 2 * s.proj), BF16),
                wide,
                wide,
                pltpu.VMEM((s.flat, 2 * s.proj), F32),
            ],
            [pltpu.with_memory_space_constraint(x, pltpu.HBM) for x in params],
            scratch=[pltpu.VMEM(x.shape, F32) for x in params]
            + [pltpu.SemaphoreType.DMA((len(params),))],
            inputs=pl.ANY,
        ),
    )
    common = [q, g, w_both, lse, corr]
    total_shape = pltpu.VMEM((s.wide, s.two), F32)
    dq_shape = pltpu.VMEM((rows, s.wide, s.proj), F32)
    own_shape = pltpu.VMEM((s.flat, width), F32)
    term_shape = pltpu.VMEM((s.flat + 16, width), BF16)

    def score(members, pairs, own):
        grid = pltpu.VMEM((pairs, rows, s.wide, s.two), F32)
        outs = call(
            functools.partial(scores, s=s, pairs=pairs, own=own),
            [pltpu.VMEM((2, pairs, rows, s.two, s.proj), BF16), grid, grid],
            [place, *common, *members],
            scratch=[pltpu.VMEM((pairs, rows, s.two, 2 * s.proj), F32)],
            scalar=True,
        )
        return [here(x) for x in outs]

    sets = [*score([kv, blocks[0]], 1, True), *score(blocks[1:], nrow - 1, False)]
    ends = pltpu.VMEM((nrow // 2, s.wide, s.two), F32)
    own, *terms, send, keep, dq = call(
        functools.partial(back, s=s, nrow=nrow),
        [own_shape] + [term_shape] * (ncol - 1) + [ends, ends, dq_shape],
        [place, *common[:3], *groups, *sets],
        scratch=[
            pltpu.VMEM((nrow, s.wide, s.two), BF16),
            pltpu.VMEM((nrow, rows, s.two, width), F32),
            pltpu.VMEM((nrow, s.wide, s.two), F32),
        ],
        scalar=True,
    )
    got = [here(move(terms[k - 1], "col", ncol, k)) for k in range(1, ncol)]
    swapped = here(move(send, "sub", nsub, 1))
    summed, *sums = call(
        functools.partial(middle, s=s, nrow=nrow),
        [total_shape] + [pltpu.VMEM((s.wide // 2 + 16, s.two), BF16)] * (nrow - 1),
        [here(keep), swapped],
    )
    dgot = [here(move(sums[k - 1], "row", nrow, k)) for k in range(1, nrow)]
    part = jax.ShapeDtypeStruct((rows, cols, width), F32)
    (query_grad,) = call(functools.partial(tail, s=s), [part], [here(dq), wq])
    key_grad, bias_grad = call(
        functools.partial(finish, s=s, ncol=ncol, nrow=nrow),
        [pltpu.HBM((rows, cols, width), F32), pltpu.HBM((heads, cols, cols), F32)],
        [here(own), here(summed), *got, *dgot],
        scratch=[
            pltpu.VMEM((rows, cols, width), F32),
            pltpu.VMEM((heads, cols, cols), F32),
            pltpu.SemaphoreType.DMA((2,)),
        ],
        outputs=pl.ANY,
    )
    return query_grad, key_grad, bias_grad


def solution(mesh):
    size = mesh.shape
    placed = (
        P(("groups", "row", "sub"), "col", None),
        P(),
        P(),
        P(),
        P("groups", "col", ("row", "sub")),
        P(("groups", "row", "sub"), "col", None),
        P(None, ("groups", "row", "sub"), "col"),
        P(None, ("groups", "row", "sub"), "col"),
    )
    return jax.shard_map(
        functools.partial(on_device, size["col"], size["row"], size["sub"]),
        mesh=mesh,
        in_specs=placed,
        out_specs=(
            P(("groups", "row", "sub"), "col", None),
            P(("groups", "row", "sub"), "col", None),
            P("groups", "col", ("row", "sub")),
        ),
        check_vma=False,
    )
```

```python
import functools

import jax
import jax.numpy as jnp
from jax import lax
from jax.experimental import pallas as pl
from jax.experimental.pallas import tpu as pltpu
from jax.sharding import PartitionSpec as P

NN = (((1,), (0,)), ((), ()))
NT = (((1,), (1,)), ((), ()))
TN = (((0,), (0,)), ((), ()))
F32 = jnp.float32
BF16 = jnp.bfloat16
LEVEL = 235.0


def split(x):
    high = x.astype(BF16)
    return high, (x - high.astype(F32)).astype(BF16)


def one(x, y, dims):
    return lax.dot_general(x, y, dims, preferred_element_type=F32)


def dot3(a, b, dims):
    axis = 0 if dims is NT else 1
    size = b[0].shape[axis]
    both = one(a[0], jnp.concatenate(b, axis=axis), dims)
    return both[:, :size] + both[:, size:] + one(a[1], b[0], dims)


def pair_of(ref, *index):
    return ref[(0, *index)], ref[(1, *index)]


def store(ref, pieces, *index):
    ref[(0, *index)] = pieces[0]
    ref[(1, *index)] = pieces[1]


class Shape:
    def __init__(self, rows, cols, width, heads, head_dim):
        self.rows, self.cols, self.width = rows, cols, width
        self.heads, self.head_dim = heads, head_dim
        self.proj, self.wide = heads * head_dim, heads * cols
        self.flat, self.two = rows * cols, 2 * cols


def encode(ref, x):
    rows, lanes = x.shape
    peak = jnp.max(jnp.max(jnp.abs(x), axis=1, keepdims=True), axis=0, keepdims=True)
    top = jnp.maximum(peak, 1e-30).astype(BF16)
    z = x * (LEVEL / top.astype(F32))
    z2 = z * z
    z4 = z2 * z2
    z8 = z4 * z4
    z16 = z8 * z8
    ref[0:rows] = jnp.where(x < 0, -z16, z16).astype(BF16)
    ref[rows : rows + 16] = jnp.broadcast_to(top, (16, lanes))


def decode(ref):
    rows = ref.shape[0] - 16
    code = ref[0:rows].astype(F32)
    top = ref[rows : rows + 16].astype(F32)[0:1]
    size = jnp.exp2(jnp.log2(jnp.abs(code)) * 0.0625)
    return jnp.where(code < 0, -size, size) * (top * (1.0 / LEVEL))


def half_join(low, high, width):
    lane = lax.broadcasted_iota(jnp.int32, low.shape, 1)
    return jnp.where(lane < width, low, high)


def pack(own_ref, other_ref, out_ref, *, s):
    out_ref[:, 0 : s.cols] = own_ref[...].reshape(s.wide, s.cols)
    out_ref[:, s.cols : s.two] = other_ref[...].reshape(s.wide, s.cols)


def prep(*refs, s):
    sources, outs = refs[:7], refs[7:14]
    buffers, sem = refs[14:21], refs[21]
    copies = [pltpu.make_async_copy(src, dst, sem.at[i]) for i, (src, dst) in enumerate(zip(sources, buffers))]
    for copy in copies:
        copy.start()
    for copy in copies:
        copy.wait()
    pair_ref, wq_ref, wk_ref, wv_ref, grad_ref, lse_ref, corr_ref = buffers
    q_out, g_out, wq_out, w_out, lse_out, corr_out, kv_out = outs
    wq = split(wq_ref[...])
    both = split(jnp.concatenate([wk_ref[...], wv_ref[...]], axis=1))
    store(wq_out, wq)
    store(w_out, both)
    own = split(pair_ref[...].reshape(s.flat, s.width))
    query = split(dot3(own, wq, NN) * (s.head_dim ** (-0.5)))
    kv_out[...] = dot3(own, both, NN)
    grads = split(grad_ref[...].reshape(s.flat, s.proj))
    row_head = lax.broadcasted_iota(jnp.int32, (s.wide, s.proj), 0) // s.cols
    chan_head = lax.broadcasted_iota(jnp.int32, (s.wide, s.proj), 1) // s.head_dim
    diag = row_head == chan_head

    def spread(piece):
        return jnp.where(diag, jnp.concatenate([piece] * s.heads, axis=0), jnp.zeros((), piece.dtype))

    def widen(ref, row):
        stack = jnp.concatenate([ref[head, row : row + 1, :] for head in range(s.heads)], axis=0)
        stack = jnp.concatenate([stack, jnp.zeros((8 - s.heads % 8, s.cols), F32)], axis=0)
        turned = stack.T
        return jnp.concatenate(
            [jnp.broadcast_to(turned[:, head : head + 1], (s.cols, s.two)) for head in range(s.heads)], axis=0
        )

    for r in range(s.rows):
        rows = slice(r * s.cols, (r + 1) * s.cols)
        store(q_out, [spread(x[rows]) for x in query], r)
        store(g_out, [spread(x[rows]) for x in grads], r)
        lse_out[r] = widen(lse_ref, r)
        corr_out[r] = widen(corr_ref, r)


def from_block(s, ref):
    return lambda both: dot3(split(ref[...].reshape(s.flat, s.width)), both, NN)


def scores(where_ref, *refs, s, pairs, own):
    q_ref, g_ref, w_ref, lse_ref, corr_ref = refs[:5]
    blocks = refs[5 : 5 + 2 * pairs]
    key_out, score_out, cot_out, kv_scr = refs[5 + 2 * pairs :]
    both = pair_of(w_ref)
    odd = where_ref[0] & 1
    for p in range(pairs):
        for slot in range(2):
            ref = blocks[2 * p + slot]
            value = ref[...] if own and p == 0 and slot == 0 else from_block(s, ref)(both)
            for r in range(s.rows):
                kv_scr[p, r, pl.ds((odd ^ slot) * s.cols, s.cols)] = value[r * s.cols : (r + 1) * s.cols]
        for r in range(s.rows):
            key = split(kv_scr[p, r, :, 0 : s.proj])
            val = split(kv_scr[p, r, :, s.proj : 2 * s.proj])
            store(key_out, key, p, r)
            score_out[p, r] = dot3(pair_of(q_ref, r), key, NT) - lse_ref[r]
            cot_out[p, r] = dot3(pair_of(g_ref, r), val, NT) - corr_ref[r]


def back(where_ref, *refs, s, nrow):
    q_ref, g_ref, w_ref = refs[:3]
    groups = refs[3 : 3 + nrow]
    sets = [refs[3 + nrow : 6 + nrow], refs[6 + nrow : 9 + nrow]]
    outs = refs[9 + nrow :]
    own_out, terms_out = outs[0], outs[1 : 2 * nrow]
    send_out, keep_out, dq_out, bias_scr, term_scr, spot = outs[2 * nrow :]
    shift = where_ref[0]
    odd = shift & 1
    both = pair_of(w_ref)
    for m, ref in enumerate(groups):
        bias_scr[m] = ref[...]
    dquery = [None] * s.rows
    for p in range(nrow):
        key_ref, score_ref, cot_ref = sets[min(p, 1)]
        at = max(p - 1, 0)
        group = (shift >> 1) ^ p
        bias = bias_scr[group].astype(F32)
        total = None
        grads = []
        for r in range(s.rows):
            query = pair_of(q_ref, r)
            cot = pair_of(g_ref, r)
            probs = jnp.exp(score_ref[at, r] + bias)
            ds = probs * cot_ref[at, r]
            total = ds if total is None else total + ds
            dsp = split(ds)
            part = dot3(dsp, pair_of(key_ref, at, r), NN)
            dquery[r] = part if dquery[r] is None else dquery[r] + part
            grads.append(jnp.concatenate([dot3(dsp, query, TN), dot3(split(probs), cot, TN)], axis=1))
        spot[group] = total
        term = dot3(split(jnp.concatenate(grads, axis=0)), both, NT)
        term_scr[p] = term.reshape(s.rows, s.two, s.width)
        for slot in range(2):
            value = jnp.concatenate(
                [term_scr[p, r, pl.ds((odd ^ slot) * s.cols, s.cols)] for r in range(s.rows)], axis=0
            )
            if p == 0 and slot == 0:
                own_out[...] = value
            else:
                encode(terms_out[2 * p + slot - 1], value)
    for r in range(s.rows):
        dq_out[r] = dquery[r]
    for p in range(nrow // 2):
        low, high = spot[2 * p], spot[2 * p + 1]
        keep_out[p] = half_join(low, pltpu.roll(high, s.cols, 1), s.cols)
        send_out[p] = half_join(pltpu.roll(low, s.cols, 1), high, s.cols)


def middle(keep_ref, got_ref, *outs, s, nrow):
    half = s.wide // 2
    for m in range(nrow):
        total = keep_ref[m // 2] + got_ref[m // 2]
        if m == 0:
            outs[0][...] = total
            continue
        top, bottom = total[:half], total[half:]
        if m % 2:
            top = pltpu.roll(top, s.cols, 1)
        else:
            bottom = pltpu.roll(bottom, s.cols, 1)
        encode(outs[m], half_join(top, bottom, s.cols))


def tail(dq_ref, wq_ref, out_ref, *, s):
    fold_mask = lax.broadcasted_iota(jnp.int32, (s.cols, s.proj), 1) // s.head_dim
    rows = []
    for r in range(s.rows):
        out = dq_ref[r, 0 : s.cols]
        for head in range(1, s.heads):
            out = jnp.where(fold_mask == head, dq_ref[r, head * s.cols : (head + 1) * s.cols], out)
        rows.append(out)
    dq = jnp.concatenate(rows, axis=0) * (s.head_dim ** (-0.5))
    out_ref[...] = dot3(split(dq), pair_of(wq_ref), NT).reshape(s.rows, s.cols, s.width)


def gather_up(own_ref, *refs):
    total = own_ref[...]
    for ref in refs[:-1]:
        total = total + decode(ref)
    refs[-1][...] = total


def finish(own_ref, sum_ref, *refs, s, nrow):
    terms, parts = refs[:1], refs[1:nrow]
    key_hbm, bias_hbm, key_out, bias_out, sem = refs[nrow:]
    total = own_ref[...]
    for ref in terms:
        total = total + decode(ref)
    key_out[...] = total.reshape(s.rows, s.cols, s.width)
    key_copy = pltpu.make_async_copy(key_out, key_hbm, sem.at[0])
    key_copy.start()
    total = None
    for ref in parts:
        value = decode(ref)
        total = value if total is None else total + value
    half = s.wide // 2
    whole = sum_ref[...]
    whole = jnp.concatenate([whole[:half] + total, whole[half:] + pltpu.roll(total, s.cols, 1)], axis=0)
    for head in range(s.heads):
        bias_out[head] = whole[head * s.cols : (head + 1) * s.cols, 0 : s.cols]
    bias_copy = pltpu.make_async_copy(bias_out, bias_hbm, sem.at[1])
    bias_copy.start()
    key_copy.wait()
    bias_copy.wait()


def xor_pairs(size, mask):
    return [(i, i ^ mask) for i in range(size)]


def here(x):
    return pltpu.with_memory_space_constraint(x, pltpu.VMEM)


def call(body, outs, args, scratch=(), scalar=False, inputs=pltpu.VMEM, outputs=pltpu.VMEM):
    specs = [pl.BlockSpec(memory_space=inputs)] * len(args)
    if scalar:
        specs[0] = pl.BlockSpec(memory_space=pltpu.SMEM)
    return pl.pallas_call(
        body,
        out_shape=outs,
        in_specs=specs,
        out_specs=[pl.BlockSpec(memory_space=outputs)] * len(outs),
        scratch_shapes=list(scratch),
        compiler_params=pltpu.CompilerParams(vmem_limit_bytes=16 << 20),
    )(*args)


def on_device(ncol, nrow, nsub, pair, w_query, w_key, w_value, bias, grad_out, log_total, row_corr):
    if nsub != 2 or ncol != 2 * nrow:
        raise ValueError("mesh shape")
    rows, cols, width = pair.shape
    heads = log_total.shape[0]
    s = Shape(rows, cols, width, heads, w_query.shape[1] // heads)

    def move(x, axis, size, mask):
        return lax.ppermute(x, axis, xor_pairs(size, mask))

    blocks = [here(move(pair, "col", ncol, k)) for k in range(1, ncol)]
    other = here(move(bias, "sub", nsub, 1))
    (packed,) = call(functools.partial(pack, s=s), [pltpu.VMEM((s.wide, s.two), BF16)], [here(bias), other])
    groups = [here(packed)] + [here(move(packed, "row", nrow, k)) for k in range(1, nrow)]
    place = lax.axis_index("col") ^ (lax.axis_index("row") * nsub + lax.axis_index("sub"))
    place = place.reshape(1)
    spread = pltpu.VMEM((2, rows, s.wide, s.proj), BF16)
    wide = pltpu.VMEM((rows, s.wide, s.two), F32)
    params = [pair, w_query, w_key, w_value, grad_out, log_total, row_corr]
    q, g, wq, w_both, lse, corr, kv = map(
        here,
        call(
            functools.partial(prep, s=s),
            [
                spread,
                spread,
                pltpu.VMEM((2, width, s.proj), BF16),
                pltpu.VMEM((2, width, 2 * s.proj), BF16),
                wide,
                wide,
                pltpu.VMEM((s.flat, 2 * s.proj), F32),
            ],
            [pltpu.with_memory_space_constraint(x, pltpu.HBM) for x in params],
            scratch=[pltpu.VMEM(x.shape, F32) for x in params]
            + [pltpu.SemaphoreType.DMA((len(params),))],
            inputs=pl.ANY,
        ),
    )
    common = [q, g, w_both, lse, corr]
    total_shape = pltpu.VMEM((s.wide, s.two), F32)
    dq_shape = pltpu.VMEM((rows, s.wide, s.proj), F32)
    own_shape = pltpu.VMEM((s.flat, width), F32)
    term_shape = pltpu.VMEM((s.flat + 16, width), BF16)

    def score(members, pairs, own):
        grid = pltpu.VMEM((pairs, rows, s.wide, s.two), F32)
        outs = call(
            functools.partial(scores, s=s, pairs=pairs, own=own),
            [pltpu.VMEM((2, pairs, rows, s.two, s.proj), BF16), grid, grid],
            [place, *common, *members],
            scratch=[pltpu.VMEM((pairs, rows, s.two, 2 * s.proj), F32)],
            scalar=True,
        )
        return [here(x) for x in outs]

    sets = [*score([kv, blocks[0]], 1, True), *score(blocks[1:], nrow - 1, False)]
    ends = pltpu.VMEM((nrow // 2, s.wide, s.two), F32)
    own, *terms, send, keep, dq = call(
        functools.partial(back, s=s, nrow=nrow),
        [own_shape] + [term_shape] * (ncol - 1) + [ends, ends, dq_shape],
        [place, *common[:3], *groups, *sets],
        scratch=[
            pltpu.VMEM((nrow, s.wide, s.two), BF16),
            pltpu.VMEM((nrow, rows, s.two, width), F32),
            pltpu.VMEM((nrow, s.wide, s.two), F32),
        ],
        scalar=True,
    )
    got = [here(move(terms[k - 1], "col", ncol, k)) for k in range(1, ncol)]
    swapped = here(move(send, "sub", nsub, 1))
    summed, *sums = call(
        functools.partial(middle, s=s, nrow=nrow),
        [total_shape] + [pltpu.VMEM((s.wide // 2 + 16, s.two), BF16)] * (nrow - 1),
        [here(keep), swapped],
    )
    dgot = [here(move(sums[k - 1], "row", nrow, k)) for k in range(1, nrow)]
    part = jax.ShapeDtypeStruct((rows, cols, width), F32)
    (query_grad,) = call(functools.partial(tail, s=s), [part], [here(dq), wq])
    (most,) = call(gather_up, [own_shape], [here(own), *got[1:]])
    key_grad, bias_grad = call(
        functools.partial(finish, s=s, nrow=nrow),
        [pltpu.HBM((rows, cols, width), F32), pltpu.HBM((heads, cols, cols), F32)],
        [here(most), here(summed), got[0], *dgot],
        scratch=[
            pltpu.VMEM((rows, cols, width), F32),
            pltpu.VMEM((heads, cols, cols), F32),
            pltpu.SemaphoreType.DMA((2,)),
        ],
        outputs=pl.ANY,
    )
    return query_grad, key_grad, bias_grad


def solution(mesh):
    size = mesh.shape
    placed = (
        P(("groups", "row", "sub"), "col", None),
        P(),
        P(),
        P(),
        P("groups", "col", ("row", "sub")),
        P(("groups", "row", "sub"), "col", None),
        P(None, ("groups", "row", "sub"), "col"),
        P(None, ("groups", "row", "sub"), "col"),
    )
    return jax.shard_map(
        functools.partial(on_device, size["col"], size["row"], size["sub"]),
        mesh=mesh,
        in_specs=placed,
        out_specs=(
            P(("groups", "row", "sub"), "col", None),
            P(("groups", "row", "sub"), "col", None),
            P("groups", "col", ("row", "sub")),
        ),
        check_vma=False,
    )
```

```python
import functools

import jax
import jax.numpy as jnp
from jax import lax
from jax.experimental import pallas as pl
from jax.experimental.pallas import tpu as pltpu
from jax.sharding import PartitionSpec as P

NN = (((1,), (0,)), ((), ()))
NT = (((1,), (1,)), ((), ()))
TN = (((0,), (0,)), ((), ()))
F32 = jnp.float32
BF16 = jnp.bfloat16
LEVEL = 235.0


def split(x):
    high = x.astype(BF16)
    return high, (x - high.astype(F32)).astype(BF16)


def one(x, y, dims):
    return lax.dot_general(x, y, dims, preferred_element_type=F32)


def dot3(a, b, dims):
    axis = 0 if dims is NT else 1
    size = b[0].shape[axis]
    both = one(a[0], jnp.concatenate(b, axis=axis), dims)
    return both[:, :size] + both[:, size:] + one(a[1], b[0], dims)


def dot3_plain(a, b, dims):
    return one(a[0], b[0], dims) + one(a[0], b[1], dims) + one(a[1], b[0], dims)


def pair_of(ref, *index):
    return ref[(0, *index)], ref[(1, *index)]


def store(ref, pieces, *index):
    ref[(0, *index)] = pieces[0]
    ref[(1, *index)] = pieces[1]


class Shape:
    def __init__(self, rows, cols, width, heads, head_dim):
        self.rows, self.cols, self.width = rows, cols, width
        self.heads, self.head_dim = heads, head_dim
        self.proj, self.wide = heads * head_dim, heads * cols
        self.flat, self.two = rows * cols, 2 * cols


def encode(ref, x):
    rows, lanes = x.shape
    peak = jnp.max(jnp.max(jnp.abs(x), axis=1, keepdims=True), axis=0, keepdims=True)
    top = jnp.maximum(peak, 1e-30).astype(BF16)
    z = x * (LEVEL / top.astype(F32))
    z2 = z * z
    z4 = z2 * z2
    z8 = z4 * z4
    z16 = z8 * z8
    ref[0:rows] = jnp.where(x < 0, -z16, z16).astype(BF16)
    ref[rows : rows + 16] = jnp.broadcast_to(top, (16, lanes))


def decode(ref):
    rows = ref.shape[0] - 16
    code = ref[0:rows].astype(F32)
    top = ref[rows : rows + 16].astype(F32)[0:1]
    size = jnp.exp2(jnp.log2(jnp.abs(code)) * 0.0625)
    return jnp.where(code < 0, -size, size) * (top * (1.0 / LEVEL))


def half_join(low, high, width):
    lane = lax.broadcasted_iota(jnp.int32, low.shape, 1)
    return jnp.where(lane < width, low, high)


def pack(own_ref, other_ref, out_ref, *, s):
    out_ref[:, 0 : s.cols] = own_ref[...].reshape(s.wide, s.cols)
    out_ref[:, s.cols : s.two] = other_ref[...].reshape(s.wide, s.cols)


def prep(*refs, s):
    sources, outs = refs[:7], refs[7:14]
    buffers, sem = refs[14:21], refs[21]
    copies = [pltpu.make_async_copy(src, dst, sem.at[i]) for i, (src, dst) in enumerate(zip(sources, buffers))]
    for copy in copies:
        copy.start()
    for copy in copies:
        copy.wait()
    pair_ref, wq_ref, wk_ref, wv_ref, grad_ref, lse_ref, corr_ref = buffers
    q_out, g_out, wq_out, w_out, lse_out, corr_out, kv_out = outs
    wq = split(wq_ref[...])
    both = split(jnp.concatenate([wk_ref[...], wv_ref[...]], axis=1))
    store(wq_out, wq)
    store(w_out, both)
    own = split(pair_ref[...].reshape(s.flat, s.width))
    query = split(dot3(own, wq, NN) * (s.head_dim ** (-0.5)))
    kv_out[...] = dot3(own, both, NN)
    grads = split(grad_ref[...].reshape(s.flat, s.proj))
    row_head = lax.broadcasted_iota(jnp.int32, (s.wide, s.proj), 0) // s.cols
    chan_head = lax.broadcasted_iota(jnp.int32, (s.wide, s.proj), 1) // s.head_dim
    diag = row_head == chan_head

    def spread(piece):
        return jnp.where(diag, jnp.concatenate([piece] * s.heads, axis=0), jnp.zeros((), piece.dtype))

    def widen(ref, row):
        stack = jnp.concatenate([ref[head, row : row + 1, :] for head in range(s.heads)], axis=0)
        stack = jnp.concatenate([stack, jnp.zeros((8 - s.heads % 8, s.cols), F32)], axis=0)
        turned = stack.T
        return jnp.concatenate(
            [jnp.broadcast_to(turned[:, head : head + 1], (s.cols, s.two)) for head in range(s.heads)], axis=0
        )

    for r in range(s.rows):
        rows = slice(r * s.cols, (r + 1) * s.cols)
        store(q_out, [spread(x[rows]) for x in query], r)
        store(g_out, [spread(x[rows]) for x in grads], r)
        lse_out[r] = widen(lse_ref, r)
        corr_out[r] = widen(corr_ref, r)


def from_block(s, ref):
    return lambda both: dot3_plain(split(ref[...].reshape(s.flat, s.width)), both, NN)


def scores(where_ref, *refs, s, pairs, own):
    q_ref, g_ref, w_ref, lse_ref, corr_ref = refs[:5]
    blocks = refs[5 : 5 + 2 * pairs]
    key_out, score_out, cot_out, kv_scr = refs[5 + 2 * pairs :]
    both = pair_of(w_ref)
    odd = where_ref[0] & 1
    for p in range(pairs):
        for slot in range(2):
            ref = blocks[2 * p + slot]
            value = ref[...] if own and p == 0 and slot == 0 else from_block(s, ref)(both)
            for r in range(s.rows):
                kv_scr[p, r, pl.ds((odd ^ slot) * s.cols, s.cols)] = value[r * s.cols : (r + 1) * s.cols]
        for r in range(s.rows):
            key = split(kv_scr[p, r, :, 0 : s.proj])
            val = split(kv_scr[p, r, :, s.proj : 2 * s.proj])
            store(key_out, key, p, r)
            score_out[p, r] = dot3_plain(pair_of(q_ref, r), key, NT) - lse_ref[r]
            cot_out[p, r] = dot3_plain(pair_of(g_ref, r), val, NT) - corr_ref[r]


def back(where_ref, *refs, s, nrow):
    q_ref, g_ref, w_ref = refs[:3]
    groups = refs[3 : 3 + nrow]
    sets = [refs[3 + nrow : 6 + nrow], refs[6 + nrow : 9 + nrow]]
    outs = refs[9 + nrow :]
    own_out, terms_out = outs[0], outs[1 : 2 * nrow]
    send_out, keep_out, dq_out, bias_scr, term_scr, spot = outs[2 * nrow :]
    shift = where_ref[0]
    odd = shift & 1
    both = pair_of(w_ref)
    for m, ref in enumerate(groups):
        bias_scr[m] = ref[...]
    dquery = [None] * s.rows
    for p in range(nrow):
        key_ref, score_ref, cot_ref = sets[min(p, 1)]
        at = max(p - 1, 0)
        group = (shift >> 1) ^ p
        bias = bias_scr[group].astype(F32)
        total = None
        grads = []
        for r in range(s.rows):
            query = pair_of(q_ref, r)
            cot = pair_of(g_ref, r)
            probs = jnp.exp(score_ref[at, r] + bias)
            ds = probs * cot_ref[at, r]
            total = ds if total is None else total + ds
            dsp = split(ds)
            part = dot3(dsp, pair_of(key_ref, at, r), NN)
            dquery[r] = part if dquery[r] is None else dquery[r] + part
            grads.append(jnp.concatenate([dot3(dsp, query, TN), dot3(split(probs), cot, TN)], axis=1))
        spot[group] = total
        term = dot3(split(jnp.concatenate(grads, axis=0)), both, NT)
        term_scr[p] = term.reshape(s.rows, s.two, s.width)
        for slot in range(2):
            value = jnp.concatenate(
                [term_scr[p, r, pl.ds((odd ^ slot) * s.cols, s.cols)] for r in range(s.rows)], axis=0
            )
            if p == 0 and slot == 0:
                own_out[...] = value
            else:
                encode(terms_out[2 * p + slot - 1], value)
    for r in range(s.rows):
        dq_out[r] = dquery[r]
    for p in range(nrow // 2):
        low, high = spot[2 * p], spot[2 * p + 1]
        keep_out[p] = half_join(low, pltpu.roll(high, s.cols, 1), s.cols)
        send_out[p] = half_join(pltpu.roll(low, s.cols, 1), high, s.cols)


def middle(keep_ref, got_ref, *outs, s, nrow):
    half = s.wide // 2
    for m in range(nrow):
        total = keep_ref[m // 2] + got_ref[m // 2]
        if m == 0:
            outs[0][...] = total
            continue
        top, bottom = total[:half], total[half:]
        if m % 2:
            top = pltpu.roll(top, s.cols, 1)
        else:
            bottom = pltpu.roll(bottom, s.cols, 1)
        encode(outs[m], half_join(top, bottom, s.cols))


def tail(dq_ref, wq_ref, out_ref, *, s):
    fold_mask = lax.broadcasted_iota(jnp.int32, (s.cols, s.proj), 1) // s.head_dim
    rows = []
    for r in range(s.rows):
        out = dq_ref[r, 0 : s.cols]
        for head in range(1, s.heads):
            out = jnp.where(fold_mask == head, dq_ref[r, head * s.cols : (head + 1) * s.cols], out)
        rows.append(out)
    dq = jnp.concatenate(rows, axis=0) * (s.head_dim ** (-0.5))
    out_ref[...] = dot3(split(dq), pair_of(wq_ref), NT).reshape(s.rows, s.cols, s.width)


def gather_up(own_ref, *refs):
    total = own_ref[...]
    for ref in refs[:-1]:
        total = total + decode(ref)
    refs[-1][...] = total


def finish(own_ref, sum_ref, *refs, s, nrow):
    terms, parts = refs[:1], refs[1:nrow]
    key_hbm, bias_hbm, key_out, bias_out, sem = refs[nrow:]
    total = own_ref[...]
    for ref in terms:
        total = total + decode(ref)
    key_out[...] = total.reshape(s.rows, s.cols, s.width)
    key_copy = pltpu.make_async_copy(key_out, key_hbm, sem.at[0])
    key_copy.start()
    total = None
    for ref in parts:
        value = decode(ref)
        total = value if total is None else total + value
    half = s.wide // 2
    whole = sum_ref[...]
    whole = jnp.concatenate([whole[:half] + total, whole[half:] + pltpu.roll(total, s.cols, 1)], axis=0)
    for head in range(s.heads):
        bias_out[head] = whole[head * s.cols : (head + 1) * s.cols, 0 : s.cols]
    bias_copy = pltpu.make_async_copy(bias_out, bias_hbm, sem.at[1])
    bias_copy.start()
    key_copy.wait()
    bias_copy.wait()


def xor_pairs(size, mask):
    return [(i, i ^ mask) for i in range(size)]


def here(x):
    return pltpu.with_memory_space_constraint(x, pltpu.VMEM)


def call(body, outs, args, scratch=(), scalar=False, inputs=pltpu.VMEM, outputs=pltpu.VMEM):
    specs = [pl.BlockSpec(memory_space=inputs)] * len(args)
    if scalar:
        specs[0] = pl.BlockSpec(memory_space=pltpu.SMEM)
    return pl.pallas_call(
        body,
        out_shape=outs,
        in_specs=specs,
        out_specs=[pl.BlockSpec(memory_space=outputs)] * len(outs),
        scratch_shapes=list(scratch),
        compiler_params=pltpu.CompilerParams(vmem_limit_bytes=16 << 20),
    )(*args)


def on_device(ncol, nrow, nsub, pair, w_query, w_key, w_value, bias, grad_out, log_total, row_corr):
    if nsub != 2 or ncol != 2 * nrow:
        raise ValueError("mesh shape")
    rows, cols, width = pair.shape
    heads = log_total.shape[0]
    s = Shape(rows, cols, width, heads, w_query.shape[1] // heads)

    def move(x, axis, size, mask):
        return lax.ppermute(x, axis, xor_pairs(size, mask))

    blocks = [here(move(pair, "col", ncol, k)) for k in range(1, ncol)]
    other = here(move(bias, "sub", nsub, 1))
    (packed,) = call(functools.partial(pack, s=s), [pltpu.VMEM((s.wide, s.two), BF16)], [here(bias), other])
    groups = [here(packed)] + [here(move(packed, "row", nrow, k)) for k in range(1, nrow)]
    place = lax.axis_index("col") ^ (lax.axis_index("row") * nsub + lax.axis_index("sub"))
    place = place.reshape(1)
    spread = pltpu.VMEM((2, rows, s.wide, s.proj), BF16)
    wide = pltpu.VMEM((rows, s.wide, s.two), F32)
    params = [pair, w_query, w_key, w_value, grad_out, log_total, row_corr]
    q, g, wq, w_both, lse, corr, kv = map(
        here,
        call(
            functools.partial(prep, s=s),
            [
                spread,
                spread,
                pltpu.VMEM((2, width, s.proj), BF16),
                pltpu.VMEM((2, width, 2 * s.proj), BF16),
                wide,
                wide,
                pltpu.VMEM((s.flat, 2 * s.proj), F32),
            ],
            [pltpu.with_memory_space_constraint(x, pltpu.HBM) for x in params],
            scratch=[pltpu.VMEM(x.shape, F32) for x in params]
            + [pltpu.SemaphoreType.DMA((len(params),))],
            inputs=pl.ANY,
        ),
    )
    common = [q, g, w_both, lse, corr]
    total_shape = pltpu.VMEM((s.wide, s.two), F32)
    dq_shape = pltpu.VMEM((rows, s.wide, s.proj), F32)
    own_shape = pltpu.VMEM((s.flat, width), F32)
    term_shape = pltpu.VMEM((s.flat + 16, width), BF16)

    def score(members, pairs, own):
        grid = pltpu.VMEM((pairs, rows, s.wide, s.two), F32)
        outs = call(
            functools.partial(scores, s=s, pairs=pairs, own=own),
            [pltpu.VMEM((2, pairs, rows, s.two, s.proj), BF16), grid, grid],
            [place, *common, *members],
            scratch=[pltpu.VMEM((pairs, rows, s.two, 2 * s.proj), F32)],
            scalar=True,
        )
        return [here(x) for x in outs]

    sets = [*score([kv, blocks[0]], 1, True), *score(blocks[1:], nrow - 1, False)]
    ends = pltpu.VMEM((nrow // 2, s.wide, s.two), F32)
    own, *terms, send, keep, dq = call(
        functools.partial(back, s=s, nrow=nrow),
        [own_shape] + [term_shape] * (ncol - 1) + [ends, ends, dq_shape],
        [place, *common[:3], *groups, *sets],
        scratch=[
            pltpu.VMEM((nrow, s.wide, s.two), BF16),
            pltpu.VMEM((nrow, rows, s.two, width), F32),
            pltpu.VMEM((nrow, s.wide, s.two), F32),
        ],
        scalar=True,
    )
    got = [here(move(terms[k - 1], "col", ncol, k)) for k in range(1, ncol)]
    swapped = here(move(send, "sub", nsub, 1))
    summed, *sums = call(
        functools.partial(middle, s=s, nrow=nrow),
        [total_shape] + [pltpu.VMEM((s.wide // 2 + 16, s.two), BF16)] * (nrow - 1),
        [here(keep), swapped],
    )
    dgot = [here(move(sums[k - 1], "row", nrow, k)) for k in range(1, nrow)]
    part = jax.ShapeDtypeStruct((rows, cols, width), F32)
    (query_grad,) = call(functools.partial(tail, s=s), [part], [here(dq), wq])
    (most,) = call(gather_up, [own_shape], [here(own), *got[1:]])
    key_grad, bias_grad = call(
        functools.partial(finish, s=s, nrow=nrow),
        [pltpu.HBM((rows, cols, width), F32), pltpu.HBM((heads, cols, cols), F32)],
        [here(most), here(summed), got[0], *dgot],
        scratch=[
            pltpu.VMEM((rows, cols, width), F32),
            pltpu.VMEM((heads, cols, cols), F32),
            pltpu.SemaphoreType.DMA((2,)),
        ],
        outputs=pl.ANY,
    )
    return query_grad, key_grad, bias_grad


def solution(mesh):
    size = mesh.shape
    placed = (
        P(("groups", "row", "sub"), "col", None),
        P(),
        P(),
        P(),
        P("groups", "col", ("row", "sub")),
        P(("groups", "row", "sub"), "col", None),
        P(None, ("groups", "row", "sub"), "col"),
        P(None, ("groups", "row", "sub"), "col"),
    )
    return jax.shard_map(
        functools.partial(on_device, size["col"], size["row"], size["sub"]),
        mesh=mesh,
        in_specs=placed,
        out_specs=(
            P(("groups", "row", "sub"), "col", None),
            P(("groups", "row", "sub"), "col", None),
            P("groups", "col", ("row", "sub")),
        ),
        check_vma=False,
    )
```
